128 devices in a mesh: ctx: 32 (over z, y_lo, x), head: 4 (over y_hi, core).
Axes of the slice: x: 4, y: 4 (y_hi: 2, y_lo: 2; y = y_hi * 2 + y_lo), z: 4, core: 2. Of those that a mesh axis runs over, the one named last changes fastest.
Arguments:
- events: bfloat16 [24576, 1024], P('ctx', 'head'), may hold values from -3 to 3
- norm_gain: float32 [1024], replicated, may hold values from 0.5 to 1.5
- w_uvqk: bfloat16 [1024, 4, 1024], P(None, None, 'head'), may hold values from -4 to 4
- w_out: bfloat16 [1024, 1024], P('head'), may hold values from -0.1875 to 0.1875
- lengths: int32 [8], replicated, may hold values from 1 to 13824, 24576 in all
Outputs:
- mixed: bfloat16 [24576, 1024], P('ctx', 'head')
The draws below stay inside these ranges and needn't reach their ends.
Inputs may be any that keep to these rules, and one draw needn't show every extreme that they name: The lengths sum to 24576; the longest is exactly 13824.
All inputs are finite; a program needn't handle non-finite values.
Results may differ from the reference program's by a relative error of at most 0.0062.
Values may be sent and summed in bfloat16 or wider, within the bound.
No kernel may reach another device: no remote copies, remote signals or barrier semaphores. Data moves between devices by JAX's collectives and lax.ppermute only.
A program may use at most 128 MiB of HBM per device.

```python
import math
import jax
import jax.numpy as jnp
import numpy as np
from jax import lax

D = 1024
HEADS = 8
HDIM = 128
TOK_DEV = 768
SEQS = 8
TOKENS = 24576
LMAX = 13824


def pattern_prototype():
    hidden_entry = jnp.arange(D, dtype=jnp.int32)
    pattern_array = hidden_entry % 8 == 0
    polarity_entries = jnp.where(hidden_entry % 16 == 0, 1.0, -1.0).astype(jnp.float32)
    return (pattern_array, polarity_entries)


def draw_events(key, part):
    jitter_key, amp_key, period_key, shift_key = jax.random.split(key, 4)
    jitter = jax.random.truncated_normal(jitter_key, -3.0, 3.0, (TOKENS, D), jnp.float32)
    amplitude = jax.random.uniform(amp_key, (4, D), jnp.float32, 0.4, 1.0)
    period = TOK_DEV * jnp.exp(jax.random.uniform(period_key, (4, D), jnp.float32, math.log(1.5), math.log(12.0)))
    phase_shift = jax.random.uniform(shift_key, (4, D), jnp.float32, -math.pi, math.pi)
    position = jnp.arange(TOKENS, dtype=jnp.float32)
    smooth = jnp.zeros((TOKENS, D), jnp.float32)
    for term_index in range(4):
        angle_rate = 2.0 * math.pi / period[term_index]
        smooth = smooth + amplitude[term_index][None, :] * jnp.sin(position[:, None] * angle_rate[None, :] + phase_shift[term_index][None, :])
    pattern_array, polarity_entries = pattern_prototype()
    baseline_strength = jnp.where(pattern_array, 0.8 * polarity_entries, 0.0).astype(jnp.float32)
    return (0.25 * (jitter + smooth) + baseline_strength[None, :]).astype(jnp.bfloat16)


def draw_w_uvqk(key, part):
    base_key, spread_key = jax.random.split(key)
    factor = D ** (-0.5)
    base = jax.random.truncated_normal(base_key, -4.0, 4.0, (D, 4, D), jnp.float32)
    spread = jax.random.uniform(spread_key, (D, 4, D), jnp.float32, 0.5, 1.5)
    pattern_array, polarity_entries = pattern_prototype()
    column_scale = jnp.array([1.0, 2.0, 6.0, 4.0], jnp.float32)
    displacement_size = jnp.array([0.0, -0.64, 0.0, -2.26], jnp.float32)
    noise_part = factor * column_scale[None, :, None] * base
    modulated_entries = 8.0 / D * polarity_entries[:, None, None] * displacement_size[None, :, None] * spread
    modulate_input = pattern_array[:, None, None] & (displacement_size != 0.0)[None, :, None]
    return jnp.where(modulate_input, modulated_entries, noise_part).astype(jnp.bfloat16)


def shard_levels(rng, extent, shards, low, largest):
    def one(dim, parts):
        draws = jax.random.uniform(jax.random.fold_in(jax.random.fold_in(rng, 6), dim), (parts,), jnp.float32, low / len(shards), largest / len(shards))
        return jnp.repeat(jnp.exp(draws), extent[dim] // parts).reshape((-1,) + (1,) * (len(extent) - dim - 1))

    loudness = one(*shards[0])
    for cut in shards[1:]:
        loudness = loudness * one(*cut)
    return loudness


def profile(amount, total, reach, slope):
    loads = [(1 << 20) // math.isqrt(standing ** slope) + 1 for standing in range(2, amount + 1)]
    spare, given = total - reach - (amount - 1), [1] * (amount - 1)
    while spare > 0:
        candidates = [i for i in range(amount - 1) if given[i] < reach]
        mass, left = sum([loads[i] for i in candidates]), spare
        for i in candidates:
            extra = min(reach - given[i], max(1, left * loads[i] // mass), spare)
            given[i] = given[i] + extra
            spare = spare - extra
    return np.array([reach] + given)


def uneven_parts(stream_key, amount, total, bound, skew):
    if amount == 2:
        one = jax.random.randint(stream_key, (), max(1, total - bound), min(bound, total - 1) + 1)
        return jnp.stack([one, total - one])
    tallies = jnp.asarray(profile(amount, total, bound, skew), jnp.int32)
    couples = (amount - 1) // 2
    source_of, receiver = tallies[1:1 + 2 * couples:2], tallies[2:2 + 2 * couples:2]
    margin = jnp.minimum(source_of - 1, bound - receiver)
    moved = jax.random.randint(jax.random.fold_in(stream_key, 1), (couples,), 0, 1 << 20) % (margin + 1)
    tallies = tallies.at[1:1 + 2 * couples:2].set(source_of - moved).at[2:2 + 2 * couples:2].set(receiver + moved)
    return tallies[jax.random.permutation(jax.random.fold_in(stream_key, 2), amount)]


def noise(key, extent, scale, most, cuts=(), held_as=jnp.bfloat16):
    values = jax.random.normal(key, extent, jnp.float32) * scale
    if len(cuts) > 0:
        values = shard_levels(key, extent, cuts, -0.22, 0.18) * values
    return jnp.clip(values, min=-most, max=most).astype(held_as)


def setup_inputs(seed: int = 0) -> dict:
    keys = jax.random.split(jax.random.key(seed), 6)
    return {
        "events": draw_events(jax.random.fold_in(keys[5], 71), 0),
        "norm_gain": jnp.clip(1.0 + 0.1 * jax.random.normal(keys[1], (D,), jnp.float32), 0.5, 1.5),
        "w_uvqk": draw_w_uvqk(jax.random.fold_in(keys[5], 71), 0),
        "w_out": noise(keys[3], (D, D), D ** -0.5, 0.1875, ((0, 4),)),
        "lengths": uneven_parts(keys[4], SEQS, TOKENS, LMAX, 2).astype(jnp.int32),
    }


def reference(events, norm_gain, w_uvqk, w_out, lengths):
    epsilon = 1e-05
    xfloat = events.astype(jnp.float32)
    row_mean = lax.optimization_barrier(jnp.mean(xfloat, axis=-1, keepdims=True))
    centered = xfloat - row_mean
    row_var = lax.optimization_barrier(jnp.mean(centered * centered, axis=-1, keepdims=True))
    normed = (centered * lax.rsqrt(row_var + epsilon) * norm_gain).astype(jnp.bfloat16)
    projected = jax.nn.silu(jnp.dot(normed, w_uvqk.reshape(D, 4 * D), preferred_element_type=jnp.float32)).astype(jnp.bfloat16)
    projected = projected.reshape(TOKENS, 4, HEADS, HDIM)
    gate_rows = projected[:, 0]
    value_rows = projected[:, 1].astype(jnp.float32)
    query_rows = projected[:, 2].astype(jnp.float32)
    key_rows = projected[:, 3].astype(jnp.float32)
    seq_ends = jnp.cumsum(lengths).astype(jnp.int32)
    positions = jnp.arange(TOKENS, dtype=jnp.int32)
    segment = lax.optimization_barrier(jnp.sum((positions[:, None] >= seq_ends[None, :]).astype(jnp.int32), axis=1))
    score_scale = HDIM ** (-0.5)
    block_size = math.gcd(TOKENS, 256)
    block_count = TOKENS // block_size

    def one_block(block_index):
        first_row = (block_index * block_size).astype(jnp.int32)
        queries = lax.dynamic_slice_in_dim(query_rows, first_row, block_size, 0)
        query_pos = first_row + jnp.arange(block_size, dtype=jnp.int32)
        query_seg = lax.dynamic_slice_in_dim(segment, first_row, block_size, 0)
        scores = jnp.einsum('qhd,khd->hqk', queries, key_rows) * score_scale
        allowed = (query_seg[:, None] == segment[None, :]) & (positions[None, :] <= query_pos[:, None])
        weights = jnp.where(allowed[None], jax.nn.silu(scores), 0.0).astype(jnp.bfloat16)
        return jnp.einsum('hqk,khd->qhd', weights.astype(jnp.float32), value_rows)
    attended = lax.map(one_block, jnp.arange(block_count, dtype=jnp.int32)).reshape(TOKENS, HEADS, HDIM)
    squares = lax.optimization_barrier(jnp.sum(attended * attended, axis=(1, 2)))
    inverse_rms = lax.rsqrt(squares / D + epsilon)
    gated = (attended * inverse_rms[:, None, None] * gate_rows.astype(jnp.float32)).astype(jnp.bfloat16).reshape(TOKENS, D)
    mixed = xfloat + jnp.dot(gated, w_out, preferred_element_type=jnp.float32)
    return mixed.astype(jnp.bfloat16)
```

```python
import jax
import jax.numpy as jnp
import numpy as np
from jax import lax
from jax.experimental import pallas as pl
from jax.experimental.pallas import tpu as pltpu
from jax.sharding import Mesh
from jax.sharding import PartitionSpec as P

D = 1024
HDIM = 128
ROWS = 768
SUB = 384
EPS = 1e-05
AXES = ("z", "yl", "x", "yh", "core")
SIZES = (4, 2, 4, 2, 2)
HALF_SCALE = 0.5 * HDIM ** (-0.5)
BF = jnp.bfloat16
F32 = jnp.float32


def send(array, target):
    pairs = []
    for source in range(int(np.prod(SIZES))):
        place = np.unravel_index(source, SIZES)
        dest = [int(t) % n for t, n in zip(target(*[int(p) for p in place]), SIZES)]
        pairs.append((source, int(np.ravel_multi_index(dest, SIZES))))
    return lax.ppermute(array, AXES, pairs)


def flip_core(array):
    return send(array, lambda z, yl, x, yh, c: (z, yl, x, yh, 1 - c))


def to_p1(array):
    return send(array, lambda z, yl, x, yh, c: (z, 1 - yl, x, yh, c))


def to_p2(array):
    return send(array, lambda z, yl, x, yh, c: (z, 1 - yl, x, 1 - yh, c))


def to_p3(array):
    return send(array, lambda z, yl, x, yh, c: (z, yl, x, 1 - yh, c))


def shift_z(array, d):
    return send(array, lambda z, yl, x, yh, c: (z + d, yl, x, yh, c))


def shift_x(array, d):
    return send(array, lambda z, yl, x, yh, c: (z, yl, x + d, yh, c))


def silu_of_half(h):
    return h + h * jnp.tanh(h)


PROJ_ROWS = 256


def project_kernel(*refs):
    blocks, gain_ref, w_ref = refs[:8], refs[8], refs[9]
    gate_ref, q_ref, kv_ref = refs[10:]

    def run(parts):
        xs = [r[...].astype(F32) for r in parts]
        total = sum(jnp.sum(v, axis=1, keepdims=True) for v in xs)
        mean = total * (1.0 / D)
        xs = [v - mean for v in xs]
        var = sum(jnp.sum(v * v, axis=1, keepdims=True) for v in xs) * (1.0 / D)
        inv = lax.rsqrt(var + EPS)
        acc = None
        for j, v in enumerate(xs):
            n = (v * inv * gain_ref[j : j + 1, :]).astype(BF)
            part = jnp.dot(n, w_ref[j], preferred_element_type=F32)
            acc = part if acc is None else acc + part
        y = silu_of_half(acc * 0.5).astype(BF)
        gate_ref[...] = y[:, :128]
        q_ref[...] = y[:, 256:384]
        kv_ref[:, :128] = y[:, 384:]
        kv_ref[:, 128:] = y[:, 128:256]

    step = pl.program_id(0)

    @pl.when(step < 3)
    def _():
        run(blocks[:4])

    @pl.when(step >= 3)
    def _():
        run(blocks[4:])


def project(own, other, gain, w):
    n = ROWS // PROJ_ROWS
    rows = lambda width: pl.BlockSpec((PROJ_ROWS, width), lambda i: (i, 0))
    first = pl.BlockSpec((PROJ_ROWS, 256), lambda i: (jnp.minimum(i, n - 1), 0))
    second = pl.BlockSpec((PROJ_ROWS, 256), lambda i: (jnp.maximum(i - n, 0), 0))
    return pl.pallas_call(
        project_kernel,
        grid=(2 * n,),
        in_specs=[first] * 4
        + [second] * 4
        + [pl.BlockSpec((4, 256), lambda i: (0, 0)), pl.BlockSpec((4, 256, 512), lambda i: (0, 0, 0))],
        out_specs=[rows(128), rows(128), rows(256)],
        out_shape=[
            jax.ShapeDtypeStruct((2 * ROWS, 128), BF),
            jax.ShapeDtypeStruct((2 * ROWS, 128), BF),
            jax.ShapeDtypeStruct((2 * ROWS, 256), BF),
        ],
        name="project",
    )(*own, *other, gain, w)


def attend_kernel(info, *refs):
    q_refs, kv_refs = refs[0:4], refs[4:8]
    o_refs = refs[8:12]
    kv, acc, sem = refs[12:]
    z, yl, x = info[0], info[1], info[2]
    copies = []
    for d in range(4):
        for rel in range(2):
            block = lax.rem(z - d + 4, 4) * 2 + (yl ^ rel)
            copies.append(
                pltpu.make_async_copy(
                    kv_refs[d].at[pl.ds(rel * ROWS, ROWS)],
                    kv.at[pl.ds(pl.multiple_of(block * ROWS, ROWS), ROWS)],
                    sem.at[2 * d + rel],
                )
            )
    for c in copies:
        c.start()
    for c in copies:
        c.wait()

    def start_of(position):
        s = jnp.int32(0)
        for i in range(8):
            e = info[3 + i]
            s = jnp.maximum(s, jnp.where(e <= position, e, 0))
        return s

    def tiles_upto(position):
        t = position - x * ROWS
        m = lax.div(t, 4 * ROWS)
        r = t - m * (4 * ROWS)
        count = 2 * m + 1 + (r >= SUB).astype(jnp.int32)
        return jnp.minimum(jnp.where(t < 0, 0, count), 16)

    for e in range(4):

        def query_tile(d, carry):
            zs = lax.rem(z - d + 4, 4)
            xs = lax.rem(x - e + 4, 4)
            first = (zs * 8 + (z >> 1) * 4 + xs) * ROWS + (z & 1) * SUB
            begin = start_of(first)
            begin_last = start_of(first + SUB - 1)
            low = tiles_upto(begin - SUB)
            high = tiles_upto(first + SUB - 1)
            at = pl.multiple_of(d * SUB, SUB)
            acc[...] = jnp.zeros((SUB, HDIM), F32)

            def key_tile(n, c):
                key_first = ((n >> 1) * 4 + x) * ROWS + (n & 1) * SUB
                where = pl.multiple_of(n * SUB, SUB)
                whole = (key_first + SUB - 1 <= first) & (key_first >= begin_last)

                def weights_of():
                    s = lax.dot_general(
                        q_refs[e][pl.ds(at, SUB), :],
                        kv[pl.ds(where, SUB), 0:HDIM],
                        (((1,), (1,)), ((), ())),
                        preferred_element_type=F32,
                    )
                    return silu_of_half(s * HALF_SCALE)

                def add(w):
                    acc[...] += jnp.dot(
                        w.astype(BF), kv[pl.ds(where, SUB), HDIM:], preferred_element_type=F32
                    )

                @pl.when(whole)
                def _():
                    add(weights_of())

                @pl.when(jnp.logical_not(whole))
                def _():
                    row = first + lax.broadcasted_iota(jnp.int32, (SUB, 1), 0)
                    begins = jnp.zeros((SUB, 1), jnp.int32)
                    for i in range(8):
                        end = info[3 + i]
                        begins = jnp.maximum(begins, jnp.where(row >= end, end, 0))
                    col = key_first + lax.broadcasted_iota(jnp.int32, (1, SUB), 1)
                    allowed = (col <= row) & (col >= begins)
                    add(jnp.where(allowed, weights_of(), 0.0))

                return c

            lax.fori_loop(low, high, key_tile, 0)
            o_refs[e][pl.ds(at, SUB), :] = acc[...].astype(o_refs[e].dtype)
            return carry

        lax.fori_loop(0, 4, query_tile, 0)


def attend(info, queries, keyvals):
    full = lambda shape: pl.BlockSpec(shape, lambda i, s: (0, 0))
    return pl.pallas_call(
        attend_kernel,
        grid_spec=pltpu.PrefetchScalarGridSpec(
            num_scalar_prefetch=1,
            grid=(1,),
            in_specs=[full((2 * ROWS, HDIM))] * 4 + [pl.BlockSpec(memory_space=pl.ANY)] * 4,
            out_specs=[full((2 * ROWS, HDIM))] * 4,
            scratch_shapes=[
                pltpu.VMEM((8 * ROWS, 2 * HDIM), BF),
                pltpu.VMEM((SUB, HDIM), F32),
                pltpu.SemaphoreType.DMA((8,)),
            ],
        ),
        out_shape=[jax.ShapeDtypeStruct((2 * ROWS, HDIM), F32 if e == 0 else BF) for e in range(4)],
        name="attend",
    )(info, *queries, *keyvals)


def finish_kernel(*refs):
    g_refs, w_ref, s_ref, ev_ref, out_ref = refs[:8], refs[8], refs[9], refs[10], refs[11]
    acc = None
    for i in range(8):
        part = jnp.dot(g_refs[i][...], w_ref[i], preferred_element_type=F32)
        acc = part if acc is None else acc + part
    inv = lax.rsqrt(s_ref[...] * (1.0 / D) + EPS)
    out_ref[...] = (ev_ref[...].astype(F32) + acc * inv).astype(BF)


def finish(gated, w, squares, events):
    rows = lambda width: pl.BlockSpec((256, width), lambda i: (i, 0))
    return pl.pallas_call(
        finish_kernel,
        grid=(ROWS // 256,),
        in_specs=[rows(128)] * 8
        + [pl.BlockSpec((8, 128, 256), lambda i: (0, 0, 0)), rows(1), rows(256)],
        out_specs=rows(256),
        out_shape=jax.ShapeDtypeStruct((ROWS, 256), BF),
        name="finish",
    )(*gated, w, squares, events)


def shards(events, norm_gain, w_uvqk, w_out, lengths):
    z, yl, x = (lax.axis_index(a).astype(jnp.int32) for a in ("z", "yl", "x"))
    o = lax.axis_index("yh").astype(jnp.int32) * 2 + lax.axis_index("core").astype(jnp.int32)
    pick = lambda a, i: lax.dynamic_index_in_dim(a, i, 0, keepdims=False)

    c0 = flip_core(events)
    p1, p2, p3 = to_p1(events), to_p2(events), to_p3(events)
    c1, c2, c3 = flip_core(p1), flip_core(p2), flip_core(p3)

    gain4 = norm_gain.reshape(4, 256)
    gain = jnp.stack([pick(gain4, o ^ j) for j in range(4)])
    w_head = lax.dynamic_slice_in_dim(w_uvqk, yl * HDIM, HDIM, 2).reshape(4, 256, 512)
    w_proj = jnp.stack([pick(w_head, o ^ j) for j in range(4)])
    out_cols = lambda j: lax.dynamic_slice_in_dim(w_out, (o ^ j) * 256, 256, 1)
    w0 = out_cols(0)
    w1 = send(out_cols(1), lambda z, yl, x, yh, c: (z, yl, x, yh, 1 - c))
    w2 = send(out_cols(2), lambda z, yl, x, yh, c: (z, yl, x, 1 - yh, c))
    w3 = send(out_cols(3), lambda z, yl, x, yh, c: (z, yl, x, 1 - yh, 1 - c))
    half = lambda w, r: lax.dynamic_slice_in_dim(w, (yl ^ r) * HDIM, HDIM, 0)
    w_fin = jnp.stack([half(w, r) for w, r in ((w0, 0), (w0, 1), (w2, 1), (w2, 0), (w1, 0), (w1, 1), (w3, 1), (w3, 0))])

    gate, q, kv = project((events, c0, p3, c3), (p1, c1, p2, c2), gain, w_proj)

    q4 = q.reshape(4, SUB, HDIM)
    spot = lambda d: lax.rem(z + d + 4, 4) ^ (2 * yl)
    pieces = [pick(q4, spot(0))] + [shift_z(pick(q4, spot(d)), d) for d in (1, 2, 3)]
    q_mine = jnp.concatenate(pieces, axis=0)
    queries = [q_mine] + [shift_x(q_mine, e) for e in (1, 2, 3)]
    keyvals = [kv] + [shift_z(kv, d) for d in (1, 2, 3)]

    info = jnp.concatenate([jnp.stack([z, yl, x]), jnp.cumsum(lengths).astype(jnp.int32)])
    parts = attend(info, queries, keyvals)
    total = parts[0]
    for e in (1, 2, 3):
        total = total + shift_x(parts[e], -e).astype(F32)
    total = total.astype(BF).reshape(4, SUB, HDIM)
    back = jnp.stack([total[0]] + [shift_z(total[d], -d) for d in (1, 2, 3)])
    attended = jnp.stack([pick(back, lax.rem((i ^ (2 * yl)) - z + 4, 4)) for i in range(4)])
    attended = attended.astype(F32).reshape(2, ROWS, HDIM)
    squares = jnp.sum(attended * attended, axis=2)
    gated = (attended * gate.astype(F32).reshape(2, ROWS, HDIM)).astype(BF)

    g0, s0 = gated[0], squares[0]
    g1, g2, g3 = to_p1(gated[1]), to_p2(gated[1]), to_p3(gated[0])
    s = s0 + to_p1(squares[1]) + to_p2(squares[1]) + to_p3(squares[0])
    s = s + flip_core(s)
    gs = [g0, g1, g2, g3]
    gs = gs + [flip_core(g) for g in gs]
    return finish(gs, w_fin, s.reshape(ROWS, 1), events)


def solution(mesh):
    fine = Mesh(mesh.devices.reshape(SIZES), AXES)
    ctx, head = ("z", "yl", "x"), ("yh", "core")
    in_specs = (P(ctx, head), P(), P(None, None, head), P(head, None), P())
    return jax.shard_map(shards, mesh=fine, in_specs=in_specs, out_specs=P(ctx, head), check_vma=False)
```

```python
import jax
import jax.numpy as jnp
import numpy as np
from jax import lax
from jax.experimental import pallas as pl
from jax.experimental.pallas import tpu as pltpu
from jax.sharding import Mesh
from jax.sharding import PartitionSpec as P

D = 1024
HDIM = 128
ROWS = 768
SUB = 384
TILES = 16
TAIL = 16
EPS = 1e-05
AXES = ("z", "yl", "x", "yh", "core")
SIZES = (4, 2, 4, 2, 2)
HALF_SCALE = 0.5 * HDIM ** (-0.5)
FAR = 1 << 24
BF = jnp.bfloat16
F32 = jnp.float32


def send(array, target):
    pairs = []
    for source in range(int(np.prod(SIZES))):
        place = np.unravel_index(source, SIZES)
        dest = [int(t) % n for t, n in zip(target(*[int(p) for p in place]), SIZES)]
        pairs.append((source, int(np.ravel_multi_index(dest, SIZES))))
    return lax.ppermute(array, AXES, pairs)


def flip_core(array):
    return send(array, lambda z, yl, x, yh, c: (z, yl, x, yh, 1 - c))


def to_p1(array):
    return send(array, lambda z, yl, x, yh, c: (z, 1 - yl, x, yh, c))


def to_p2(array):
    return send(array, lambda z, yl, x, yh, c: (z, 1 - yl, x, 1 - yh, c))


def to_p3(array):
    return send(array, lambda z, yl, x, yh, c: (z, yl, x, 1 - yh, c))


def shift_z(array, d):
    return send(array, lambda z, yl, x, yh, c: (z + d, yl, x, yh, c))


def shift_x(array, d):
    return send(array, lambda z, yl, x, yh, c: (z, yl, x + d, yh, c))


def silu_of_half(h):
    return h + h * jnp.tanh(h)


def whole(shape):
    return pl.BlockSpec(shape, lambda i, s: (0,) * len(shape))


def pack_weights(info, w_ref, w_vmem, groups):
    for j in range(4):
        rows = pl.ds(pl.multiple_of((info[3] ^ j) * 256, 256), 256)
        for k, g in enumerate(groups):
            cols = pl.ds(pl.multiple_of(g * 256 + info[1] * HDIM, HDIM), HDIM)
            w_vmem[j * 256 : (j + 1) * 256, k * HDIM : (k + 1) * HDIM] = w_ref[rows, cols]


def query_kernel(info, *refs):
    blocks, gain_ref, w_ref = refs[:8], refs[8], refs[9]
    q_refs, n_ref, w_vmem = refs[10:14], refs[14], refs[15]
    step = pl.program_id(0)

    @pl.when(step == 0)
    def _():
        pack_weights(info, w_ref, w_vmem, (2,))

    def run(parts):
        xs = [r[...].astype(F32) for r in parts]
        total = sum(jnp.sum(v, axis=1, keepdims=True) for v in xs)
        mean = total * (1.0 / D)
        xs = [v - mean for v in xs]
        var = sum(jnp.sum(v * v, axis=1, keepdims=True) for v in xs) * (1.0 / D)
        inv = lax.rsqrt(var + EPS)
        for j, v in enumerate(xs):
            gain = gain_ref[pl.ds(info[3] ^ j, 1), :]
            n_ref[:, j * 256 : (j + 1) * 256] = (v * inv * gain).astype(BF)

    @pl.when(step < 2)
    def _():
        run(blocks[:4])

    @pl.when(step >= 2)
    def _():
        run(blocks[4:])

    acc = jnp.dot(n_ref[...], w_vmem[...], preferred_element_type=F32)
    y = silu_of_half(acc * 0.5).astype(BF)
    shift = lax.rem((step ^ (2 * info[1])) - info[0] + 4, 4)
    for d in range(4):

        @pl.when(shift == d)
        def _():
            q_refs[d][...] = y


def project_queries(info, own, other, gain, w):
    first = pl.BlockSpec((SUB, 256), lambda i, s: (jnp.minimum(i, 1), 0))
    second = pl.BlockSpec((SUB, 256), lambda i, s: (jnp.maximum(i - 2, 0), 0))
    out = pl.pallas_call(
        query_kernel,
        grid_spec=pltpu.PrefetchScalarGridSpec(
            num_scalar_prefetch=1,
            grid=(4,),
            in_specs=[first] * 4 + [second] * 4 + [whole((4, 256)), whole((D, D))],
            out_specs=[whole((SUB, HDIM))] * 4 + [pl.BlockSpec((SUB, D), lambda i, s: (i, 0))],
            scratch_shapes=[pltpu.VMEM((D, HDIM), BF)],
        ),
        out_shape=[jax.ShapeDtypeStruct((SUB, HDIM), BF)] * 4 + [jax.ShapeDtypeStruct((2 * ROWS, D), BF)],
        name="project_queries",
    )(info, *own, *other, gain, w)
    return out[:4], out[4]


def rest_kernel(info, n_ref, w_ref, gate_ref, kv_ref, w_vmem):
    @pl.when(pl.program_id(0) == 0)
    def _():
        pack_weights(info, w_ref, w_vmem, (3, 1, 0))

    acc = jnp.dot(n_ref[...], w_vmem[...], preferred_element_type=F32)
    y = silu_of_half(acc * 0.5).astype(BF)
    kv_ref[...] = y[:, : 2 * HDIM]
    gate_ref[...] = y[:, 2 * HDIM :]


def project_rest(info, normed, w):
    rows = lambda width: pl.BlockSpec((SUB, width), lambda i, s: (i, 0))
    return pl.pallas_call(
        rest_kernel,
        grid_spec=pltpu.PrefetchScalarGridSpec(
            num_scalar_prefetch=1,
            grid=(4,),
            in_specs=[rows(D), whole((D, D))],
            out_specs=[rows(HDIM), rows(2 * HDIM)],
            scratch_shapes=[pltpu.VMEM((D, 3 * HDIM), BF)],
        ),
        out_shape=[
            jax.ShapeDtypeStruct((2 * ROWS, HDIM), BF),
            jax.ShapeDtypeStruct((2 * ROWS, 2 * HDIM), BF),
        ],
        name="project_rest",
    )(info, normed, w)


def attend_body(info, q_refs, kv_parts, late, q, kv, acc, full_list, edge_list, sem, more=()):
    z, yl, x = info[0], info[1], info[2]
    copies = list(more)
    for e in range(4):
        for d in range(4):
            tile = lax.rem(z - d + 4, 4) * 4 + lax.rem(x - e + 4, 4)
            copies.append(
                pltpu.make_async_copy(
                    q_refs[e].at[pl.ds(d * SUB, SUB)],
                    q.at[pl.ds(pl.multiple_of(tile * SUB, SUB), SUB)],
                    sem.at[4 * e + d],
                )
            )
    for k, (ref, row, d, rel) in enumerate(kv_parts):
        block = lax.rem(z - d + 4, 4) * 2 + (yl ^ rel)
        copies.append(
            pltpu.make_async_copy(
                ref.at[pl.ds(row, ROWS)],
                kv.at[pl.ds(pl.multiple_of(block * ROWS, ROWS), ROWS)],
                sem.at[16 + k],
            )
        )
    for c in copies:
        c.start()

    def start_of(position):
        s = jnp.int32(0)
        for i in range(8):
            e = info[4 + i]
            s = jnp.maximum(s, jnp.where(e <= position, e, 0))
        return s

    def tiles_upto(position):
        t = position - x * ROWS
        m = lax.div(t, 4 * ROWS)
        r = t - m * (4 * ROWS)
        count = 2 * m + 1 + (r >= SUB).astype(jnp.int32)
        return jnp.minimum(jnp.where(t < 0, 0, count), TILES)

    def query_first(t):
        return ((t >> 2) * 8 + (z >> 1) * 4 + (t & 3)) * ROWS + (z & 1) * SUB

    def key_first_of(n):
        return ((n >> 1) * 4 + x) * ROWS + (n & 1) * SUB

    far = lax.rem(z + 2, 4)

    def list_queries(t, counts):
        first = query_first(t)
        begin_last = start_of(first + SUB - 1)
        low = tiles_upto(start_of(first) - SUB)
        high = tiles_upto(first + SUB - 1)
        if late:
            low = jnp.maximum(low, far * 4)
            high = jnp.minimum(high, far * 4 + 4)

        def list_keys(n, counts):
            nf, ne = counts
            k = key_first_of(n)
            full = ((k + SUB - 1 <= first) & (k >= begin_last)).astype(jnp.int32)
            use = 1 if late else ((n >> 2) != far).astype(jnp.int32)
            entry = t * TILES + n
            full_list[nf] = entry
            edge_list[ne] = entry
            return nf + full * use, ne + (1 - full) * use

        return lax.fori_loop(low, high, list_keys, counts)

    nf, ne = lax.fori_loop(0, TILES, list_queries, (jnp.int32(0), jnp.int32(0)))
    groups = nf >> 2

    def move(i, ne):
        edge_list[ne] = full_list[i]
        return ne + 1

    ne = lax.fori_loop(groups * 4, nf, move, ne)
    edge_list[ne] = 256

    for c in copies:
        c.wait()

    def scores(entry):
        t, n = (entry >> 4) & 15, entry & 15
        q_rows = pl.ds(pl.multiple_of(t * SUB, SUB), SUB)
        k_rows = pl.ds(pl.multiple_of(n * SUB, SUB), SUB)
        s = lax.dot_general(
            q[q_rows, :], kv[k_rows, 0:HDIM], (((1,), (1,)), ((), ())), preferred_element_type=F32
        )
        return silu_of_half(s * HALF_SCALE), q_rows, k_rows, t, n

    def add(w, q_rows, k_rows):
        acc[q_rows, :] += jnp.dot(w.astype(BF), kv[k_rows, HDIM:], preferred_element_type=F32)

    def full_tiles(i, carry):
        for u in range(4):
            w, q_rows, k_rows, _, _ = scores(full_list[4 * i + u])
            add(w, q_rows, k_rows)
        return carry

    lax.fori_loop(0, groups, full_tiles, 0)

    def edge_tiles(i, carry):
        for u in range(2):
            entry = edge_list[2 * i + u]
            w, q_rows, k_rows, t, n = scores(entry)
            first = query_first(t)
            col = key_first_of(n) + lax.broadcasted_iota(jnp.int32, (1, SUB), 1)
            ends = jnp.full((1, SUB), FAR, jnp.int32)
            for j in range(8):
                e = info[4 + j]
                ends = jnp.minimum(ends, jnp.where(col < e, e, FAR))
            row = lax.broadcasted_iota(jnp.int32, (SUB, SUB), 0)
            skip = (entry >> 8) * FAR
            allowed = (row >= col + (skip - first)) & (row < ends - first)
            add(jnp.where(allowed, w, 0.0), q_rows, k_rows)
        return carry

    lax.fori_loop(0, (ne + 1) >> 1, edge_tiles, 0)


ATTEND_SCRATCH = [
    pltpu.VMEM((TILES * SUB, HDIM), BF),
    pltpu.VMEM((TILES * SUB, 2 * HDIM), BF),
    pltpu.SMEM((264,), jnp.int32),
    pltpu.SMEM((264,), jnp.int32),
    pltpu.SemaphoreType.DMA((24,)),
]
ANYWHERE = pl.BlockSpec(memory_space=pl.ANY)


def early_kernel(info, q0, q1, q2, q3, own, up, down, acc, q, kv, full_list, edge_list, sem):
    acc[...] = jnp.zeros(acc.shape, F32)
    parts = [(ref, r * ROWS, d, r) for ref, d in ((own, 0), (up, 1), (down, 3)) for r in range(2)]
    attend_body(info, (q0, q1, q2, q3), parts, False, q, kv, acc, full_list, edge_list, sem)


def attend_early(info, queries, own, up, down):
    return pl.pallas_call(
        early_kernel,
        grid_spec=pltpu.PrefetchScalarGridSpec(
            num_scalar_prefetch=1,
            grid=(1,),
            in_specs=[ANYWHERE] * 7,
            out_specs=whole((TILES * SUB, HDIM)),
            scratch_shapes=ATTEND_SCRATCH,
        ),
        out_shape=jax.ShapeDtypeStruct((TILES * SUB, HDIM), F32),
        name="attend_early",
    )(info, *queries, own, up, down)


def late_kernel(info, q0, q1, q2, q3, near, away, acc_in, out, q, kv, full_list, edge_list, sem, acc):
    more = [pltpu.make_async_copy(acc_in, acc, sem.at[23])]
    parts = [(near, 0, 2, 0), (away, 0, 2, 1)]
    attend_body(info, (q0, q1, q2, q3), parts, True, q, kv, acc, full_list, edge_list, sem, more)
    for t in range(TILES):
        out[t] = acc[t * SUB : (t + 1) * SUB, :].astype(BF)


def attend_late(info, queries, near, away, acc):
    return pl.pallas_call(
        late_kernel,
        grid_spec=pltpu.PrefetchScalarGridSpec(
            num_scalar_prefetch=1,
            grid=(1,),
            in_specs=[ANYWHERE] * 7,
            out_specs=whole((TILES, SUB, HDIM)),
            scratch_shapes=ATTEND_SCRATCH + [pltpu.VMEM((TILES * SUB, HDIM), F32)],
        ),
        out_shape=jax.ShapeDtypeStruct((TILES, SUB, HDIM), BF),
        name="attend_late",
    )(info, *queries, near, away, acc)


def gate_kernel(info, part_ref, gate_ref, own_ref, other_ref):
    ones = jnp.ones((8, HDIM), F32)
    for rel, out in ((0, own_ref), (1, other_ref)):
        high, low = [], []
        for half in range(2):
            i = 2 * rel + half
            a = i ^ (2 * info[1])
            total = part_ref[4 * a].astype(F32)
            for b in range(1, 4):
                total = total + part_ref[4 * a + b].astype(F32)
            gate = gate_ref[i * SUB : (i + 1) * SUB, :].astype(F32)
            out[half * SUB : (half + 1) * SUB, :] = (total * gate).astype(BF)
            sums = lax.dot_general(
                ones,
                total * total,
                (((1,), (1,)), ((), ())),
                precision=lax.Precision.HIGHEST,
                preferred_element_type=F32,
            )
            for c in range(SUB // HDIM):
                value = sums[0:1, c * HDIM : (c + 1) * HDIM]
                top = value.astype(BF).astype(F32)
                high.append(top)
                low.append(value - top)
        zero = jnp.zeros((4, HDIM), F32)
        out[ROWS:, :] = jnp.concatenate(high + low + [zero], axis=0).astype(BF)


def gate_rows(info, parts, gate):
    shape = jax.ShapeDtypeStruct((ROWS + TAIL, HDIM), BF)
    return pl.pallas_call(
        gate_kernel,
        grid_spec=pltpu.PrefetchScalarGridSpec(
            num_scalar_prefetch=1,
            grid=(1,),
            in_specs=[whole((TILES, SUB, HDIM)), whole((2 * ROWS, HDIM))],
            out_specs=[whole((ROWS + TAIL, HDIM))] * 2,
        ),
        out_shape=[shape, shape],
        name="gate_rows",
    )(info, parts, gate)


def finish_kernel(info, *refs):
    rows, tails, ws = refs[:8], refs[8:16], refs[16:20]
    ev_ref, out_ref = refs[20:]
    step = pl.program_id(0)
    acc = None
    for r, (j, flip) in zip(rows, ((0, 0), (0, 1), (2, 1), (2, 0), (1, 0), (1, 1), (3, 1), (3, 0))):
        at = pl.ds(pl.multiple_of((info[1] ^ flip) * HDIM, HDIM), HDIM)
        part = jnp.dot(r[...], ws[j][at, :], preferred_element_type=F32)
        acc = part if acc is None else acc + part
    tail = sum(t[...].astype(F32) for t in tails)
    squares = tail[0:6] + tail[6:12]
    inv = lax.rsqrt(squares * (1.0 / D) + EPS)
    which = lax.broadcasted_iota(jnp.int32, (6, HDIM), 0)
    eye = lax.broadcasted_iota(jnp.int32, (HDIM, HDIM), 0) == lax.broadcasted_iota(jnp.int32, (HDIM, HDIM), 1)
    for k in range(2):
        line = jnp.sum(jnp.where(which == 2 * step + k, inv, 0.0), axis=0, keepdims=True)
        column = jnp.sum(jnp.where(eye, line, 0.0), axis=1, keepdims=True)
        at = slice(k * HDIM, (k + 1) * HDIM)
        out_ref[at, :] = (ev_ref[at, :].astype(F32) + acc[at, :] * column).astype(BF)


def finish(info, gated, ws, events):
    rows = lambda width: pl.BlockSpec((256, width), lambda i, s: (i, 0))
    tail = pl.BlockSpec((TAIL, HDIM), lambda i, s: (ROWS // TAIL, 0))
    return pl.pallas_call(
        finish_kernel,
        grid_spec=pltpu.PrefetchScalarGridSpec(
            num_scalar_prefetch=1,
            grid=(ROWS // 256,),
            in_specs=[rows(HDIM)] * 8 + [tail] * 8 + [whole((256, 256))] * 4 + [rows(256)],
            out_specs=rows(256),
        ),
        out_shape=jax.ShapeDtypeStruct((ROWS, 256), BF),
        name="finish",
    )(info, *gated, *gated, *ws, events)


def shards(events, norm_gain, w_uvqk, w_out, lengths):
    z, yl, x = (lax.axis_index(a).astype(jnp.int32) for a in ("z", "yl", "x"))
    o = lax.axis_index("yh").astype(jnp.int32) * 2 + lax.axis_index("core").astype(jnp.int32)
    info = jnp.concatenate([jnp.stack([z, yl, x, o]), jnp.cumsum(lengths).astype(jnp.int32)])

    c0 = flip_core(events)
    p1, p2, p3 = to_p1(events), to_p2(events), to_p3(events)
    c1, c2, c3 = flip_core(p1), flip_core(p2), flip_core(p3)

    w_in = w_uvqk.reshape(D, 4 * 256)
    out_cols = lambda j: lax.dynamic_slice_in_dim(w_out, (o ^ j) * 256, 256, 1)
    ws = [
        out_cols(0),
        flip_core(out_cols(1)),
        to_p3(out_cols(2)),
        send(out_cols(3), lambda z, yl, x, yh, c: (z, yl, x, 1 - yh, 1 - c)),
    ]

    gain = norm_gain.reshape(4, 256)
    pieces, normed = project_queries(info, (events, c0, p3, c3), (p1, c1, p2, c2), gain, w_in)

    pieces = [pieces[0]] + [shift_z(pieces[d], d) for d in (1, 2, 3)]
    gate, kv = project_rest(info, normed, w_in)
    q_mine = jnp.concatenate(pieces, axis=0)
    queries = [q_mine] + [shift_x(q_mine, e) for e in (1, 2, 3)]

    up, down = shift_z(kv, 1), shift_z(kv, -1)
    near, away = shift_z(up[:ROWS], 1), shift_z(down[ROWS:], -1)

    acc = attend_early(info, queries, kv, up, down)
    parts = attend_late(info, queries, near, away, acc)
    parts = lax.all_to_all(parts, ("z", "x"), 0, 0)

    own, other = gate_rows(info, parts, gate)
    gated = [own, to_p1(other), to_p2(other), to_p3(own)]
    gated = gated + [flip_core(g) for g in gated]
    return finish(info, gated, ws, events)


def solution(mesh):
    fine = Mesh(mesh.devices.reshape(SIZES), AXES)
    ctx, head = ("z", "yl", "x"), ("yh", "core")
    in_specs = (P(ctx, head), P(), P(None, None, head), P(head, None), P())
    return jax.shard_map(shards, mesh=fine, in_specs=in_specs, out_specs=P(ctx, head), check_vma=False)
```

```python
import jax
import jax.numpy as jnp
import numpy as np
from jax import lax
from jax.experimental import pallas as pl
from jax.experimental.pallas import tpu as pltpu
from jax.sharding import Mesh
from jax.sharding import PartitionSpec as P


D = 1024
HDIM = 128
ROWS = 768
SUB = 384
TILES = 16
KEYS = 256
KEY_TILES = 24
TAIL = 16
EPS = 1e-05
AXES = ("z", "yl", "x", "yh", "core")
SIZES = (4, 2, 4, 2, 2)
HALF_SCALE = 0.5 * HDIM ** (-0.5)
FAR = 1 << 24
BF = jnp.bfloat16
F32 = jnp.float32


def send(array, target):
    pairs = []
    for source in range(int(np.prod(SIZES))):
        place = np.unravel_index(source, SIZES)
        dest = [int(t) % n for t, n in zip(target(*[int(p) for p in place]), SIZES)]
        pairs.append((source, int(np.ravel_multi_index(dest, SIZES))))
    return lax.ppermute(array, AXES, pairs)


def flip_core(array):
    return send(array, lambda z, yl, x, yh, c: (z, yl, x, yh, 1 - c))


def to_p1(array):
    return send(array, lambda z, yl, x, yh, c: (z, 1 - yl, x, yh, c))


def to_p2(array):
    return send(array, lambda z, yl, x, yh, c: (z, 1 - yl, x, 1 - yh, c))


def to_p3(array):
    return send(array, lambda z, yl, x, yh, c: (z, yl, x, 1 - yh, c))


def shift_z(array, d):
    return send(array, lambda z, yl, x, yh, c: (z + d, yl, x, yh, c))


def shift_x(array, d):
    return send(array, lambda z, yl, x, yh, c: (z, yl, x + d, yh, c))


def silu_of_half(h):
    return h + h * jnp.tanh(h)


def whole(shape):
    return pl.BlockSpec(shape, lambda i, s: (0,) * len(shape))


def pack_kernel(info, w_ref, w_out):
    for j in range(4):
        rows = pl.ds(pl.multiple_of((info[3] ^ j) * 256, 256), 256)
        for k, g in enumerate((0, 1, 2, 3)):
            cols = pl.ds(pl.multiple_of(g * 256 + info[1] * HDIM, HDIM), HDIM)
            w_out[j * 256 : (j + 1) * 256, k * HDIM : (k + 1) * HDIM] = w_ref[rows, cols]


def pack_weights(info, w):
    return pl.pallas_call(
        pack_kernel,
        grid_spec=pltpu.PrefetchScalarGridSpec(
            num_scalar_prefetch=1, grid=(1,), in_specs=[whole((D, D))], out_specs=whole((D, 4 * HDIM))
        ),
        out_shape=jax.ShapeDtypeStruct((D, 4 * HDIM), BF),
        name="pack_weights",
    )(info, w)


PIECE = 128


def project_rows(info, parts, gain_ref, w_ref, put):
    for r in range(SUB // PIECE):
        at = slice(r * PIECE, (r + 1) * PIECE)
        xs = [p[at, :].astype(F32) for p in parts]
        total = sum(jnp.sum(v, axis=1, keepdims=True) for v in xs)
        mean = total * (1.0 / D)
        xs = [v - mean for v in xs]
        var = sum(jnp.sum(v * v, axis=1, keepdims=True) for v in xs) * (1.0 / D)
        inv = lax.rsqrt(var + EPS)
        acc = None
        for j, v in enumerate(xs):
            n = (v * inv * gain_ref[pl.ds(info[3] ^ j, 1), :]).astype(BF)
            part = jnp.dot(n, w_ref[j * 256 : (j + 1) * 256, :], preferred_element_type=F32)
            acc = part if acc is None else acc + part
        put(at, silu_of_half(acc * 0.5).astype(BF))


def other_kernel(info, *refs):
    blocks, gain_ref, w_ref = refs[:4], refs[4], refs[5]
    gate_ref, q_ref, kv_ref = refs[6:]

    def put(at, y):
        gate_ref[at, :] = y[:, :128]
        q_ref[at, :] = y[:, 256:384]
        kv_ref[at, :128] = y[:, 384:]
        kv_ref[at, 128:] = y[:, 128:256]

    project_rows(info, blocks, gain_ref, w_ref, put)


def own_kernel(info, *refs):
    blocks, gain_ref, w_ref, q_other = refs[:4], refs[4], refs[5], refs[6]
    gate_ref, kv_ref, q_refs, q_vmem = refs[7], refs[8], refs[9:13], refs[13]
    step = pl.program_id(0)

    def put(at, y):
        gate_ref[at, :] = y[:, :128]
        q_vmem[at, :] = y[:, 256:384]
        kv_ref[at, :128] = y[:, 384:]
        kv_ref[at, 128:] = y[:, 128:256]

    project_rows(info, blocks, gain_ref, w_ref, put)
    for rel, source in ((0, q_vmem), (1, q_other)):
        shift = lax.rem(((2 * rel + step) ^ (2 * info[1])) - info[0] + 4, 4)
        for d in range(4):

            @pl.when(shift == d)
            def _():
                q_refs[d][...] = source[...]


def project_other(info, blocks, gain, w):
    rows = lambda width: pl.BlockSpec((SUB, width), lambda i, s: (i, 0))
    return pl.pallas_call(
        other_kernel,
        grid_spec=pltpu.PrefetchScalarGridSpec(
            num_scalar_prefetch=1,
            grid=(2,),
            in_specs=[rows(256)] * 4 + [whole((4, 256)), whole((D, 4 * HDIM))],
            out_specs=[rows(HDIM), rows(HDIM), rows(2 * HDIM)],
        ),
        out_shape=[
            jax.ShapeDtypeStruct((ROWS, HDIM), BF),
            jax.ShapeDtypeStruct((ROWS, HDIM), BF),
            jax.ShapeDtypeStruct((ROWS, 2 * HDIM), BF),
        ],
        name="project_other",
    )(info, *blocks, gain, w)


def project_own(info, blocks, gain, w, q_other):
    rows = lambda width: pl.BlockSpec((SUB, width), lambda i, s: (i, 0))
    return pl.pallas_call(
        own_kernel,
        grid_spec=pltpu.PrefetchScalarGridSpec(
            num_scalar_prefetch=1,
            grid=(2,),
            in_specs=[rows(256)] * 4 + [whole((4, 256)), whole((D, 4 * HDIM)), rows(HDIM)],
            out_specs=[rows(HDIM), rows(2 * HDIM)] + [whole((SUB, HDIM))] * 4,
            scratch_shapes=[pltpu.VMEM((SUB, HDIM), BF)],
        ),
        out_shape=[
            jax.ShapeDtypeStruct((ROWS, HDIM), BF),
            jax.ShapeDtypeStruct((ROWS, 2 * HDIM), BF),
        ]
        + [jax.ShapeDtypeStruct((SUB, HDIM), BF)] * 4,
        name="project_own",
    )(info, *blocks, gain, w, q_other)


def attend_body(info, q_refs, kv_parts, late, q, kv, acc, full_list, edge_list, sem, more=()):
    z, yl, x = info[0], info[1], info[2]
    copies = list(more)
    for e, ref in q_refs:
        for d in range(4):
            tile = lax.rem(z - d + 4, 4) * 4 + lax.rem(x - e + 4, 4)
            copies.append(
                pltpu.make_async_copy(
                    ref.at[pl.ds(d * SUB, SUB)],
                    q.at[pl.ds(pl.multiple_of(tile * SUB, SUB), SUB)],
                    sem.at[4 * e + d],
                )
            )
    for k, (ref, row, d, rel) in enumerate(kv_parts):
        block = lax.rem(z - d + 4, 4) * 2 + (yl ^ rel)
        copies.append(
            pltpu.make_async_copy(
                ref.at[pl.ds(row, ROWS)],
                kv.at[pl.ds(pl.multiple_of(block * ROWS, ROWS), ROWS)],
                sem.at[16 + k],
            )
        )
    for c in copies:
        c.start()

    def start_of(position):
        s = jnp.int32(0)
        for i in range(8):
            e = info[4 + i]
            s = jnp.maximum(s, jnp.where(e <= position, e, 0))
        return s

    def tiles_upto(position):
        t = position - x * ROWS
        m = lax.div(t, 4 * ROWS)
        r = lax.div(t - m * (4 * ROWS), KEYS)
        count = 3 * m + 1 + jnp.minimum(r, 2)
        return jnp.minimum(jnp.where(t < 0, 0, count), KEY_TILES)

    def query_first(t):
        return ((t >> 2) * 8 + (z >> 1) * 4 + (t & 3)) * ROWS + (z & 1) * SUB

    def key_first_of(n):
        m = lax.div(n, 3)
        return (m * 4 + x) * ROWS + (n - 3 * m) * KEYS

    far_z, far_x = lax.rem(z + 2, 4), lax.rem(x + 2, 4)

    def list_queries(t, counts):
        first = query_first(t)
        begin_last = start_of(first + SUB - 1)
        low = tiles_upto(start_of(first) - KEYS)
        high = tiles_upto(first + SUB - 1)
        if late:
            near = (t & 3) != far_x
            low = jnp.where(near, jnp.maximum(low, far_z * 6), low)
            high = jnp.where(near, jnp.minimum(high, far_z * 6 + 6), high)
        else:
            high = jnp.where((t & 3) == far_x, low, high)

        def list_keys(n, counts):
            nf, ne = counts
            k = key_first_of(n)
            full = ((k + KEYS - 1 <= first) & (k >= begin_last)).astype(jnp.int32)
            use = 1 if late else (lax.div(n, 6) != far_z).astype(jnp.int32)
            entry = t * 32 + n
            full_list[nf] = entry
            edge_list[ne] = entry
            return nf + full * use, ne + (1 - full) * use

        return lax.fori_loop(low, high, list_keys, counts)

    nf, ne = lax.fori_loop(0, TILES, list_queries, (jnp.int32(0), jnp.int32(0)))
    groups = nf >> 2

    def move(i, ne):
        edge_list[ne] = full_list[i]
        return ne + 1

    ne = lax.fori_loop(groups * 4, nf, move, ne)
    edge_list[ne] = 512 + (z * 4 + x) * 32 + z * 6

    for c in copies:
        c.wait()

    def scores(entry):
        t, n = (entry >> 5) & 15, entry & 31
        q_rows = pl.ds(pl.multiple_of(t * SUB, SUB), SUB)
        k_rows = pl.ds(pl.multiple_of(n * KEYS, KEYS), KEYS)
        s = lax.dot_general(
            q[q_rows, :], kv[k_rows, 0:HDIM], (((1,), (1,)), ((), ())), preferred_element_type=F32
        )
        return silu_of_half(s * HALF_SCALE), q_rows, k_rows, t, n

    def add(w, q_rows, k_rows):
        acc[q_rows, :] += jnp.dot(w.astype(BF), kv[k_rows, HDIM:], preferred_element_type=F32)

    def full_tiles(i, carry):
        for u in range(4):
            w, q_rows, k_rows, _, _ = scores(full_list[4 * i + u])
            add(w, q_rows, k_rows)
        return carry

    lax.fori_loop(0, groups, full_tiles, 0)

    def edge_tiles(i, carry):
        for u in range(2):
            entry = edge_list[2 * i + u]
            w, q_rows, k_rows, t, n = scores(entry)
            first = query_first(t)
            col = key_first_of(n) + lax.broadcasted_iota(jnp.int32, (1, KEYS), 1)
            ends = jnp.full((1, KEYS), FAR, jnp.int32)
            for j in range(8):
                e = info[4 + j]
                ends = jnp.minimum(ends, jnp.where(col < e, e, FAR))
            row = lax.broadcasted_iota(jnp.int32, (SUB, KEYS), 0)
            skip = (entry >> 9) * FAR
            allowed = (row >= col + (skip - first)) & (row < ends - first)
            add(jnp.where(allowed, w, 0.0), q_rows, k_rows)
        return carry

    lax.fori_loop(0, (ne + 1) >> 1, edge_tiles, 0)


ATTEND_SCRATCH = [
    pltpu.VMEM((TILES * SUB, HDIM), BF),
    pltpu.VMEM((TILES * SUB, 2 * HDIM), BF),
    pltpu.SMEM((400,), jnp.int32),
    pltpu.SMEM((400,), jnp.int32),
    pltpu.SemaphoreType.DMA((25,)),
]
ANYWHERE = pl.BlockSpec(memory_space=pl.ANY)


def early_kernel(info, *refs):
    q_refs, kv_refs, acc = list(zip((0, 1, 3), refs[:3])), refs[3:9], refs[9]
    q, kv, full_list, edge_list, sem = refs[10:]
    acc[...] = jnp.zeros(acc.shape, F32)
    parts = [(kv_refs[2 * k + r], 0, d, r) for k, d in enumerate((0, 1, 3)) for r in range(2)]
    attend_body(info, q_refs, parts, False, q, kv, acc, full_list, edge_list, sem)


def attend_early(info, queries, keyvals):
    return pl.pallas_call(
        early_kernel,
        grid_spec=pltpu.PrefetchScalarGridSpec(
            num_scalar_prefetch=1,
            grid=(1,),
            in_specs=[ANYWHERE] * 9,
            out_specs=whole((TILES * SUB, HDIM)),
            scratch_shapes=ATTEND_SCRATCH,
        ),
        out_shape=jax.ShapeDtypeStruct((TILES * SUB, HDIM), F32),
        name="attend_early",
    )(info, *queries, *keyvals)


def late_kernel(info, *refs):
    q_refs, kv_refs, acc_in, out = list(zip((0, 1, 3, 2), refs[:4])), refs[4:12], refs[12], refs[13]
    q, kv, full_list, edge_list, sem, acc = refs[14:]
    more = [pltpu.make_async_copy(acc_in, acc, sem.at[24])]
    parts = [(kv_refs[2 * k + r], 0, d, r) for k, d in enumerate((0, 1, 3, 2)) for r in range(2)]
    attend_body(info, q_refs, parts, True, q, kv, acc, full_list, edge_list, sem, more)
    for t in range(TILES):
        out[t] = acc[t * SUB : (t + 1) * SUB, :].astype(BF)


def attend_late(info, queries, keyvals, acc):
    return pl.pallas_call(
        late_kernel,
        grid_spec=pltpu.PrefetchScalarGridSpec(
            num_scalar_prefetch=1,
            grid=(1,),
            in_specs=[ANYWHERE] * 13,
            out_specs=whole((TILES, SUB, HDIM)),
            scratch_shapes=ATTEND_SCRATCH + [pltpu.VMEM((TILES * SUB, HDIM), F32)],
        ),
        out_shape=jax.ShapeDtypeStruct((TILES, SUB, HDIM), BF),
        name="attend_late",
    )(info, *queries, *keyvals, acc)


def gate_kernel(info, part_ref, gate_own, gate_other, own_ref, other_ref):
    ones = jnp.ones((8, HDIM), F32)
    for rel, gate_ref, out in ((0, gate_own, own_ref), (1, gate_other, other_ref)):
        high, low = [], []
        for half in range(2):
            a = (2 * rel + half) ^ (2 * info[1])
            total = part_ref[4 * a].astype(F32)
            for b in range(1, 4):
                total = total + part_ref[4 * a + b].astype(F32)
            at = slice(half * SUB, (half + 1) * SUB)
            out[at, :] = (total * gate_ref[at, :].astype(F32)).astype(BF)
            sums = lax.dot_general(
                ones,
                total * total,
                (((1,), (1,)), ((), ())),
                precision=lax.Precision.HIGHEST,
                preferred_element_type=F32,
            )
            for c in range(SUB // HDIM):
                value = sums[0:1, c * HDIM : (c + 1) * HDIM]
                top = value.astype(BF).astype(F32)
                high.append(top)
                low.append(value - top)
        zero = jnp.zeros((4, HDIM), F32)
        out[ROWS:, :] = jnp.concatenate(high + low + [zero], axis=0).astype(BF)


def gate_rows(info, parts, gate_own, gate_other):
    shape = jax.ShapeDtypeStruct((ROWS + TAIL, HDIM), BF)
    return pl.pallas_call(
        gate_kernel,
        grid_spec=pltpu.PrefetchScalarGridSpec(
            num_scalar_prefetch=1,
            grid=(1,),
            in_specs=[whole((TILES, SUB, HDIM))] + [whole((ROWS, HDIM))] * 2,
            out_specs=[whole((ROWS + TAIL, HDIM))] * 2,
        ),
        out_shape=[shape, shape],
        name="gate_rows",
    )(info, parts, gate_own, gate_other)


def mix_kernel(info, *refs):
    rows, w_here, w_there = refs[:4], refs[4], refs[5]
    mine_ref, theirs_ref, squares_ref = refs[6:]
    core = info[3] & 1
    for out, c in ((theirs_ref, 1 - core), (mine_ref, core)):
        cols = pl.ds(pl.multiple_of(c * 256, 256), 256)
        acc = None
        for r, w, flip in zip(rows, (w_here, w_here, w_there, w_there), (0, 1, 1, 0)):
            at = pl.ds(pl.multiple_of((info[1] ^ flip) * HDIM, HDIM), HDIM)
            part = jnp.dot(r[0:ROWS, :], w[at, cols], preferred_element_type=F32)
            acc = part if acc is None else acc + part
        out[0:ROWS, :] = acc
    tail = sum(r[ROWS:, :].astype(F32) for r in rows)
    squares = jnp.concatenate([tail[0:6] + tail[6:12], jnp.zeros((2, HDIM), F32)], axis=0)
    squares_ref[...] = squares
    theirs_ref[ROWS:, 0:HDIM] = squares
    theirs_ref[ROWS:, HDIM:] = squares


def mix(info, gated, w_here, w_there):
    return pl.pallas_call(
        mix_kernel,
        grid_spec=pltpu.PrefetchScalarGridSpec(
            num_scalar_prefetch=1,
            grid=(1,),
            in_specs=[whole((ROWS + TAIL, HDIM))] * 4 + [whole((256, 512))] * 2,
            out_specs=[whole((ROWS, 256)), whole((ROWS + 8, 256)), whole((8, HDIM))],
        ),
        out_shape=[
            jax.ShapeDtypeStruct((ROWS, 256), F32),
            jax.ShapeDtypeStruct((ROWS + 8, 256), F32),
            jax.ShapeDtypeStruct((8, HDIM), F32),
        ],
        name="mix",
    )(info, *gated, w_here, w_there)


def finish_kernel(mine_ref, got_ref, tail_ref, squares_ref, ev_ref, out_ref):
    step = pl.program_id(0)
    inv = lax.rsqrt((squares_ref[...] + tail_ref[:, 0:HDIM]) * (1.0 / D) + EPS)
    which = lax.broadcasted_iota(jnp.int32, (8, HDIM), 0)
    eye = lax.broadcasted_iota(jnp.int32, (HDIM, HDIM), 0) == lax.broadcasted_iota(jnp.int32, (HDIM, HDIM), 1)
    for k in range(2):
        line = jnp.sum(jnp.where(which == 2 * step + k, inv, 0.0), axis=0, keepdims=True)
        column = jnp.sum(jnp.where(eye, line, 0.0), axis=1, keepdims=True)
        at = slice(k * HDIM, (k + 1) * HDIM)
        total = mine_ref[at, :] + got_ref[at, :]
        out_ref[at, :] = (ev_ref[at, :].astype(F32) + total * column).astype(BF)


def finish(mine, got, squares, events):
    rows = pl.BlockSpec((256, 256), lambda i: (i, 0))
    tail = pl.BlockSpec((8, 256), lambda i: (ROWS // 8, 0))
    return pl.pallas_call(
        finish_kernel,
        grid=(ROWS // 256,),
        in_specs=[rows, rows, tail, pl.BlockSpec((8, HDIM), lambda i: (0, 0)), rows],
        out_specs=rows,
        out_shape=jax.ShapeDtypeStruct((ROWS, 256), BF),
        name="finish",
    )(mine, got, got, squares, events)


def layer(events, norm_gain, w_uvqk, w_out, lengths):
    z, yl, x = (lax.axis_index(a).astype(jnp.int32) for a in ("z", "yl", "x"))
    yh = lax.axis_index("yh").astype(jnp.int32)
    o = yh * 2 + lax.axis_index("core").astype(jnp.int32)
    info = jnp.concatenate([jnp.stack([z, yl, x, o]), jnp.cumsum(lengths).astype(jnp.int32)])

    c0 = flip_core(events)
    p1, p2, p3 = to_p1(events), to_p2(events), to_p3(events)
    w_in = pack_weights(info, w_uvqk.reshape(D, 4 * 256))
    gain = norm_gain.reshape(4, 256)
    p1, w_in, info, gain = lax.optimization_barrier((p1, w_in, info, gain))
    c1, c2, c3 = flip_core(p1), flip_core(p2), flip_core(p3)

    gate_other, q_other, kv_other = project_other(info, (p1, c1, p2, c2), gain, w_in)
    gate_own, kv_own, *pieces = project_own(info, (events, c0, p3, c3), gain, w_in, q_other)

    pieces = [pieces[0]] + [shift_z(pieces[d], d) for d in (1, 2, 3)]
    up_other, down_other = shift_z(kv_other, 1), shift_z(kv_other, -1)
    up_own, down_own = shift_z(kv_own, 1), shift_z(kv_own, -1)

    q_mine = jnp.concatenate(pieces, axis=0)
    queries = [q_mine] + [shift_x(q_mine, e) for e in (1, 3, 2)]
    near, away = shift_z(up_own, 1), shift_z(down_other, -1)

    keyvals = [kv_own, kv_other, up_own, up_other, down_own, down_other]
    acc = attend_early(info, queries[:3], keyvals)
    parts = attend_late(info, queries, keyvals + [near, away], acc)

    w_here = lax.dynamic_slice_in_dim(w_out, yh * 512, 512, 1)
    w_away = lax.dynamic_slice_in_dim(w_out, (1 - yh) * 512, 512, 1)
    w_away, _ = lax.optimization_barrier((w_away, q_mine))
    w_there = to_p3(w_away)

    parts = lax.all_to_all(parts, ("z", "x"), 0, 0)
    own, other = gate_rows(info, parts, gate_own, gate_other)
    gated = [own, to_p1(other), to_p2(other), to_p3(own)]
    mine, theirs, squares = mix(info, gated, w_here, w_there)
    return finish(mine, flip_core(theirs), squares, events)


def solution(mesh):
    fine = Mesh(mesh.devices.reshape(SIZES), AXES)
    ctx, head = ("z", "yl", "x"), ("yh", "core")
    in_specs = (P(ctx, head), P(), P(None, None, head), P(head, None), P())
    return jax.shard_map(layer, mesh=fine, in_specs=in_specs, out_specs=P(ctx, head), check_vma=False)
```

```python
import functools

import jax
import jax.numpy as jnp
import numpy as np
from jax import lax
from jax.experimental import pallas as pl
from jax.experimental.pallas import tpu as pltpu
from jax.sharding import Mesh
from jax.sharding import PartitionSpec as P


D = 1024
HDIM = 128
ROWS = 768
SUB = 384
TILES = 16
KEYS = 256
KEY_TILES = 24
TAIL = 16
EPS = 1e-05
AXES = ("z", "yl", "x", "yh", "core")
SIZES = (4, 2, 4, 2, 2)
HALF_SCALE = 0.5 * HDIM ** (-0.5)
FAR = 1 << 24
BF = jnp.bfloat16
F32 = jnp.float32


def send(array, target):
    pairs = []
    for source in range(int(np.prod(SIZES))):
        place = np.unravel_index(source, SIZES)
        dest = [int(t) % n for t, n in zip(target(*[int(p) for p in place]), SIZES)]
        pairs.append((source, int(np.ravel_multi_index(dest, SIZES))))
    return lax.ppermute(array, AXES, pairs)


def flip_core(array):
    return send(array, lambda z, yl, x, yh, c: (z, yl, x, yh, 1 - c))


def to_p1(array):
    return send(array, lambda z, yl, x, yh, c: (z, 1 - yl, x, yh, c))


def to_p2(array):
    return send(array, lambda z, yl, x, yh, c: (z, 1 - yl, x, 1 - yh, c))


def to_p3(array):
    return send(array, lambda z, yl, x, yh, c: (z, yl, x, 1 - yh, c))


def shift_z(array, d):
    return send(array, lambda z, yl, x, yh, c: (z + d, yl, x, yh, c))


def shift_x(array, d):
    return send(array, lambda z, yl, x, yh, c: (z, yl, x + d, yh, c))


def silu_of_half(h):
    return h + h * jnp.tanh(h)


ANYWHERE = pl.BlockSpec(memory_space=pl.ANY)


def whole(shape):
    return pl.BlockSpec(shape, lambda i, *s: (0,) * len(shape))


PIECE = 128


def half_kernel(second, info, *refs):
    blocks, gain_ref, w_ref = refs[:4], refs[4], refs[5]
    if second:
        q_first, outs = refs[6], refs[11:]
    else:
        outs = refs[6:]
    gate_mine, gate_away, kv_mine, kv_away = outs[:4]
    q_refs, y = outs[4:-1], outs[-1]
    for r in range(SUB // PIECE):
        at = slice(r * PIECE, (r + 1) * PIECE)
        xs = [p[at, :].astype(F32) for p in blocks]
        total = sum(jnp.sum(v, axis=1, keepdims=True) for v in xs)
        mean = total * (1.0 / D)
        xs = [v - mean for v in xs]
        var = sum(jnp.sum(v * v, axis=1, keepdims=True) for v in xs) * (1.0 / D)
        inv = lax.rsqrt(var + EPS)
        acc = None
        for j, v in enumerate(xs):
            n = (v * inv * gain_ref[pl.ds(info[3] ^ j, 1), :]).astype(BF)
            w = w_ref[pl.ds(pl.multiple_of((info[3] ^ j) * 256, 256), 256), :]
            part = jnp.dot(n, w, preferred_element_type=F32)
            acc = part if acc is None else acc + part
        y[at, :] = silu_of_half(acc * 0.5).astype(BF)

    def columns(group, head):
        return y[:, pl.ds(pl.multiple_of(group * 256 + head * HDIM, HDIM), HDIM)]

    for gate, kv, head in ((gate_mine, kv_mine, info[1]), (gate_away, kv_away, 1 - info[1])):
        gate[...] = columns(0, head)
        kv[:, :HDIM] = columns(3, head)
        kv[:, HDIM:] = columns(1, head)
    if not second:
        for head in range(2):
            q_refs[0][head] = columns(2, head)
        return
    for half in range(2):
        for head in range(2):
            turn = info[0] ^ (2 * half + head)
            for k in range(4):

                @pl.when(turn == k)
                def _():
                    q_refs[k][...] = columns(2, head) if half else q_first[head]


def project_half(info, half, blocks, gain, w, before=()):
    part = lambda width: pl.BlockSpec((SUB, width), lambda i, s: (half, 0))
    full = lambda width: jax.ShapeDtypeStruct((ROWS, width), BF)
    widths = (HDIM, HDIM, 2 * HDIM, 2 * HDIM)
    in_specs = [part(256)] * 2 + [whole((SUB, 256))] * 2 + [whole((4, 256)), whole((D, D))]
    if half:
        in_specs = in_specs + [whole((2, SUB, HDIM))] + [ANYWHERE] * 4
        q_specs, q_shape = [whole((SUB, HDIM))] * 4, [jax.ShapeDtypeStruct((SUB, HDIM), BF)] * 4
        before = [before[4], *before[:4]]
    else:
        q_specs, q_shape = [whole((2, SUB, HDIM))], [jax.ShapeDtypeStruct((2, SUB, HDIM), BF)]
    return pl.pallas_call(
        functools.partial(half_kernel, bool(half)),
        grid_spec=pltpu.PrefetchScalarGridSpec(
            num_scalar_prefetch=1,
            grid=(1,),
            in_specs=in_specs,
            out_specs=[part(n) for n in widths] + q_specs,
            scratch_shapes=[pltpu.VMEM((SUB, D), BF)],
        ),
        out_shape=[full(n) for n in widths] + q_shape,
        input_output_aliases={8 + i: i for i in range(4)} if half else {},
        name="project_second" if half else "project_first",
    )(info, *blocks, gain, w, *before)


LIST = 416


def plan_kernel(info, full_early, edge_early, full_late, edge_late):
    z, yl, x = info[0], info[1], info[2]
    far_z, far_x = lax.rem(z + 2, 4), lax.rem(x + 2, 4)

    def start_of(position):
        s = jnp.int32(0)
        for i in range(8):
            e = info[4 + i]
            s = jnp.maximum(s, jnp.where(e <= position, e, 0))
        return s

    def tiles_upto(position):
        t = position - x * ROWS
        m = lax.div(t, 4 * ROWS)
        r = lax.div(t - m * (4 * ROWS), KEYS)
        count = 3 * m + 1 + jnp.minimum(r, 2)
        return jnp.minimum(jnp.where(t < 0, 0, count), KEY_TILES)

    def list_queries(t, counts):
        first = query_first(info, t)
        begin_last = start_of(first + SUB - 1)
        low = tiles_upto(start_of(first) - KEYS)
        high = tiles_upto(first + SUB - 1)
        near = (t & 3) != far_x

        def list_keys(n, counts):
            fe, ee, fl, el = counts
            k = key_first(info, n)
            block = lax.div(n, 3)
            bz, rel = block >> 1, (block & 1) ^ yl
            early = near & (((rel == 0) & (bz != far_z)) | (bz == z))
            full = (k + KEYS - 1 <= first) & (k >= begin_last)
            entry = t * 32 + n
            full_early[fe] = entry
            edge_early[ee] = entry
            full_late[fl] = entry
            edge_late[el] = entry
            early, full = early.astype(jnp.int32), full.astype(jnp.int32)
            return (
                fe + early * full,
                ee + early * (1 - full),
                fl + (1 - early) * full,
                el + (1 - early) * (1 - full),
            )

        return lax.fori_loop(low, high, list_keys, counts)

    zero = jnp.int32(0)
    fe, ee, fl, el = lax.fori_loop(0, TILES, list_queries, (zero, zero, zero, zero))
    for fulls, nf, edges, ne in ((full_early, fe, edge_early, ee), (full_late, fl, edge_late, el)):
        groups = nf >> 2

        def move(i, ne):
            edges[ne] = fulls[i]
            return ne + 1

        ne = lax.fori_loop(groups * 4, nf, move, ne)
        edges[ne] = 512 + (z * 4 + x) * 32 + z * 6 + 3 * yl
        fulls[LIST - 1] = groups
        edges[LIST - 1] = (ne + 1) >> 1


def query_first(info, t):
    return ((t >> 2) * 8 + (info[0] >> 1) * 4 + (t & 3)) * ROWS + (info[0] & 1) * SUB


def key_first(info, n):
    m = lax.div(n, 3)
    return (m * 4 + info[2]) * ROWS + (n - 3 * m) * KEYS


def plan(info):
    smem = pl.BlockSpec(memory_space=pltpu.SMEM)
    return pl.pallas_call(
        plan_kernel,
        grid_spec=pltpu.PrefetchScalarGridSpec(num_scalar_prefetch=1, grid=(1,), in_specs=[], out_specs=[smem] * 4),
        out_shape=[jax.ShapeDtypeStruct((LIST,), jnp.int32)] * 4,
        name="plan",
    )(info)


def attend_kernel(info, *refs):
    lists, q_refs, kv_refs, out = refs[:4], refs[4:8], refs[8:16], refs[16]
    q, kv, acc, sem = refs[17:]
    z, yl, x = info[0], info[1], info[2]

    def load_queries(e, ref):
        copies = []
        for k in range(4):
            tile = ((2 * (z & 1) + yl) ^ k) * 4 + lax.rem(x - e + 4, 4)
            copies.append(
                pltpu.make_async_copy(
                    ref.at[pl.ds(k * SUB, SUB)],
                    q.at[pl.ds(pl.multiple_of(tile * SUB, SUB), SUB)],
                    sem.at[4 * e + k],
                )
            )
        return copies

    def load_keys(k, ref, d, rel):
        block = lax.rem(z - d + 4, 4) * 2 + (yl ^ rel)
        to = kv.at[pl.ds(pl.multiple_of(block * ROWS, ROWS), ROWS)]
        return [pltpu.make_async_copy(ref, to, sem.at[16 + k])]

    queries = [load_queries(e, ref) for e, ref in zip((0, 1, 3, 2), q_refs)]
    places = zip(kv_refs, (0, 0, 1, 3, 1, 3, 2, 2), (0, 1, 0, 0, 1, 1, 0, 1))
    keys = [load_keys(k, *place) for k, place in enumerate(places)]
    early, late = sum(keys[:4] + queries[:3], []), sum(keys[4:] + queries[3:], [])
    for c in early + late:
        c.start()
    acc[...] = jnp.zeros(acc.shape, F32)
    for c in early:
        c.wait()

    def scores(entry):
        t, n = (entry >> 5) & 15, entry & 31
        q_rows = pl.ds(pl.multiple_of(t * SUB, SUB), SUB)
        k_rows = pl.ds(pl.multiple_of(n * KEYS, KEYS), KEYS)
        s = lax.dot_general(
            q[q_rows, :], kv[k_rows, 0:HDIM], (((1,), (1,)), ((), ())), preferred_element_type=F32
        )
        return silu_of_half(s * HALF_SCALE), q_rows, k_rows, t, n

    def add(w, q_rows, k_rows):
        acc[q_rows, :] += jnp.dot(w.astype(BF), kv[k_rows, HDIM:], preferred_element_type=F32)

    def run(full_list, edge_list):
        def full_tiles(i, carry):
            for u in range(4):
                w, q_rows, k_rows, _, _ = scores(full_list[4 * i + u])
                add(w, q_rows, k_rows)
            return carry

        lax.fori_loop(0, full_list[LIST - 1], full_tiles, 0)

        def edge_tiles(i, carry):
            for u in range(2):
                entry = edge_list[2 * i + u]
                w, q_rows, k_rows, t, n = scores(entry)
                first = query_first(info, t)
                col = key_first(info, n) + lax.broadcasted_iota(jnp.int32, (1, KEYS), 1)
                ends = jnp.full((1, KEYS), FAR, jnp.int32)
                for j in range(8):
                    e = info[4 + j]
                    ends = jnp.minimum(ends, jnp.where(col < e, e, FAR))
                row = lax.broadcasted_iota(jnp.int32, (SUB, KEYS), 0)
                skip = (entry >> 9) * FAR
                allowed = (row >= col + (skip - first)) & (row < ends - first)
                add(jnp.where(allowed, w, 0.0), q_rows, k_rows)
            return carry

        lax.fori_loop(0, edge_list[LIST - 1], edge_tiles, 0)

    run(lists[0], lists[1])
    for c in late:
        c.wait()
    run(lists[2], lists[3])
    for t in range(TILES):
        out[t] = acc[t * SUB : (t + 1) * SUB, :].astype(BF)


def attend(info, lists, queries, keyvals):
    return pl.pallas_call(
        attend_kernel,
        grid_spec=pltpu.PrefetchScalarGridSpec(
            num_scalar_prefetch=5,
            grid=(1,),
            in_specs=[ANYWHERE] * 12,
            out_specs=whole((TILES, SUB, HDIM)),
            scratch_shapes=[
                pltpu.VMEM((TILES * SUB, HDIM), BF),
                pltpu.VMEM((TILES * SUB, 2 * HDIM), BF),
                pltpu.VMEM((TILES * SUB, HDIM), F32),
                pltpu.SemaphoreType.DMA((24,)),
            ],
        ),
        out_shape=jax.ShapeDtypeStruct((TILES, SUB, HDIM), BF),
        name="attend",
    )(info, *lists, *queries, *keyvals)


def gate_kernel(info, part_ref, gate_mine, gate_other, own_ref, other_ref):
    step = pl.program_id(0)
    total = part_ref[0].astype(F32)
    for b in range(1, 4):
        total = total + part_ref[b].astype(F32)
    sums = lax.dot_general(
        jnp.ones((8, HDIM), F32),
        total * total,
        (((1,), (1,)), ((), ())),
        precision=lax.Precision.HIGHEST,
        preferred_element_type=F32,
    )
    for i, gate_ref, out in ((0, gate_mine, own_ref), (1, gate_mine, own_ref), (2, gate_other, other_ref), (3, gate_other, other_ref)):
        half = i & 1

        @pl.when(step == i)
        def _():
            out[half * SUB : (half + 1) * SUB, :] = (total * gate_ref[...].astype(F32)).astype(BF)
            for c in range(SUB // HDIM):
                value = sums[:, c * HDIM : (c + 1) * HDIM]
                top = value.astype(BF)
                at = ROWS + TAIL * (3 * half + c)
                out[at : at + 8, :] = top
                out[at + 8 : at + 16, :] = (value - top.astype(F32)).astype(BF)


def gate_rows(info, parts, gate_mine, gate_other):
    shape = jax.ShapeDtypeStruct((ROWS + 6 * TAIL, HDIM), BF)
    return pl.pallas_call(
        gate_kernel,
        grid_spec=pltpu.PrefetchScalarGridSpec(
            num_scalar_prefetch=1,
            grid=(4,),
            in_specs=[
                pl.BlockSpec((4, SUB, HDIM), lambda i, s: (i ^ (2 * s[1]), 0, 0)),
                pl.BlockSpec((SUB, HDIM), lambda i, s: (jnp.minimum(i, 1), 0)),
                pl.BlockSpec((SUB, HDIM), lambda i, s: (jnp.maximum(i - 2, 0), 0)),
            ],
            out_specs=[whole((ROWS + 6 * TAIL, HDIM))] * 2,
        ),
        out_shape=[shape, shape],
        name="gate_rows",
    )(info, parts, gate_mine, gate_other)


def mix_kernel(info, *refs):
    rows, w_here, w_there = refs[:4], refs[4], refs[5]
    mine_ref, theirs_ref, squares_ref = refs[6:]
    core = info[3] & 1
    for out, c in ((theirs_ref, 1 - core), (mine_ref, core)):
        cols = pl.ds(pl.multiple_of(c * 256, 256), 256)
        acc = None
        for r, w, flip in zip(rows, (w_here, w_here, w_there, w_there), (0, 1, 1, 0)):
            at = pl.ds(pl.multiple_of((info[1] ^ flip) * HDIM, HDIM), HDIM)
            part = jnp.dot(r[0:ROWS, :], w[at, cols], preferred_element_type=F32)
            acc = part if acc is None else acc + part
        out[0:ROWS, :] = acc
    tail = sum(r[ROWS:, :].astype(F32) for r in rows)
    lines = [tail[TAIL * c : TAIL * c + 1] + tail[TAIL * c + 8 : TAIL * c + 9] for c in range(6)]
    squares = jnp.concatenate(lines + [jnp.zeros((2, HDIM), F32)], axis=0)
    squares_ref[...] = squares
    theirs_ref[ROWS:, 0:HDIM] = squares
    theirs_ref[ROWS:, HDIM:] = squares


def mix(info, gated, w_here, w_there):
    return pl.pallas_call(
        mix_kernel,
        grid_spec=pltpu.PrefetchScalarGridSpec(
            num_scalar_prefetch=1,
            grid=(1,),
            in_specs=[whole((ROWS + 6 * TAIL, HDIM))] * 4 + [whole((256, 512))] * 2,
            out_specs=[whole((ROWS, 256)), whole((ROWS + 8, 256)), whole((8, HDIM))],
        ),
        out_shape=[
            jax.ShapeDtypeStruct((ROWS, 256), F32),
            jax.ShapeDtypeStruct((ROWS + 8, 256), F32),
            jax.ShapeDtypeStruct((8, HDIM), F32),
        ],
        name="mix",
    )(info, *gated, w_here, w_there)


def finish_kernel(mine_ref, got_ref, tail_ref, squares_ref, ev_ref, out_ref):
    step = pl.program_id(0)
    inv = lax.rsqrt((squares_ref[...] + tail_ref[:, 0:HDIM]) * (1.0 / D) + EPS)
    which = lax.broadcasted_iota(jnp.int32, (8, HDIM), 0)
    eye = lax.broadcasted_iota(jnp.int32, (HDIM, HDIM), 0) == lax.broadcasted_iota(jnp.int32, (HDIM, HDIM), 1)
    for k in range(2):
        line = jnp.sum(jnp.where(which == 2 * step + k, inv, 0.0), axis=0, keepdims=True)
        column = jnp.sum(jnp.where(eye, line, 0.0), axis=1, keepdims=True)
        at = slice(k * HDIM, (k + 1) * HDIM)
        total = mine_ref[at, :] + got_ref[at, :]
        out_ref[at, :] = (ev_ref[at, :].astype(F32) + total * column).astype(BF)


def finish(mine, got, squares, events):
    rows = pl.BlockSpec((256, 256), lambda i: (i, 0))
    tail = pl.BlockSpec((8, 256), lambda i: (ROWS // 8, 0))
    return pl.pallas_call(
        finish_kernel,
        grid=(ROWS // 256,),
        in_specs=[rows, rows, tail, pl.BlockSpec((8, HDIM), lambda i: (0, 0)), rows],
        out_specs=rows,
        out_shape=jax.ShapeDtypeStruct((ROWS, 256), BF),
        name="finish",
    )(mine, got, got, squares, events)


def layer(events, norm_gain, w_uvqk, w_out, lengths):
    z, yl, x = (lax.axis_index(a).astype(jnp.int32) for a in ("z", "yl", "x"))
    yh = lax.axis_index("yh").astype(jnp.int32)
    o = yh * 2 + lax.axis_index("core").astype(jnp.int32)
    info = jnp.concatenate([jnp.stack([z, yl, x, o]), jnp.cumsum(lengths).astype(jnp.int32)])

    p3 = [to_p3(events[h * SUB : (h + 1) * SUB]) for h in range(2)]
    c0 = flip_core(events)
    w_in = w_uvqk.reshape(D, 4 * 256)
    gain = norm_gain.reshape(4, 256)
    lists = plan(info)
    p3[0], w_in, info, gain, lists = lax.optimization_barrier((p3[0], w_in, info, gain, lists))
    c3 = [flip_core(p3[h]) for h in range(2)]

    first = project_half(info, 0, (events, c0, p3[0], c3[0]), gain, w_in)
    gate_mine, gate_away, kv_mine, kv_away, *pieces = project_half(
        info, 1, (events, c0, p3[1], c3[1]), gain, w_in, first
    )

    def to_class(k):
        def target(z, yl, x, yh, c):
            half, head = (z ^ k) >> 1, (z ^ k) & 1
            return 2 * yl + half, head, x, yh, c

        return target

    pieces = [send(pieces[k], to_class(k)) for k in range(4)]
    up_mine, down_mine = shift_z(kv_mine, 1), shift_z(kv_mine, -1)
    kv_other = to_p1(kv_away)
    gate_other = to_p1(gate_away)
    up_other, down_other = shift_z(kv_other, 1), shift_z(kv_other, -1)

    q_mine = jnp.concatenate(pieces, axis=0)
    queries = [q_mine] + [shift_x(q_mine, e) for e in (1, 3, 2)]
    near, away = shift_z(up_mine, 1), shift_z(down_other, -1)

    keyvals = [kv_mine, kv_other, up_mine, down_mine, up_other, down_other, near, away]
    parts = attend(info, lists, queries, keyvals)

    w_here = lax.dynamic_slice_in_dim(w_out, yh * 512, 512, 1)
    w_away = lax.dynamic_slice_in_dim(w_out, (1 - yh) * 512, 512, 1)
    w_away, _ = lax.optimization_barrier((w_away, q_mine))
    w_there = to_p3(w_away)

    parts = lax.all_to_all(parts, ("z", "x"), 0, 0)
    own, other = gate_rows(info, parts, gate_mine, gate_other)
    gated = [own, to_p1(other), to_p2(other), to_p3(own)]
    mine, theirs, squares = mix(info, gated, w_here, w_there)
    return finish(mine, flip_core(theirs), squares, events)


def solution(mesh):
    fine = Mesh(mesh.devices.reshape(SIZES), AXES)
    ctx, head = ("z", "yl", "x"), ("yh", "core")
    in_specs = (P(ctx, head), P(), P(None, None, head), P(head, None), P())
    return jax.shard_map(layer, mesh=fine, in_specs=in_specs, out_specs=P(ctx, head), check_vma=False)
```

```python
import jax
import jax.numpy as jnp
import numpy as np
from jax import lax
from jax.experimental import pallas as pl
from jax.experimental.pallas import tpu as pltpu
from jax.sharding import Mesh
from jax.sharding import PartitionSpec as P


D = 1024
HDIM = 128
ROWS = 768
SUB = 384
TILES = 16
KEYS = 256
KEY_TILES = 24
TAIL = 16
EPS = 1e-05
AXES = ("z", "yl", "x", "yh", "core")
SIZES = (4, 2, 4, 2, 2)
HALF_SCALE = 0.5 * HDIM ** (-0.5)
FAR = 1 << 24
BF = jnp.bfloat16
F32 = jnp.float32


def send(array, target):
    pairs = []
    for source in range(int(np.prod(SIZES))):
        place = np.unravel_index(source, SIZES)
        dest = [int(t) % n for t, n in zip(target(*[int(p) for p in place]), SIZES)]
        pairs.append((source, int(np.ravel_multi_index(dest, SIZES))))
    return lax.ppermute(array, AXES, pairs)


def flip_core(array):
    return send(array, lambda z, yl, x, yh, c: (z, yl, x, yh, 1 - c))


def to_p1(array):
    return send(array, lambda z, yl, x, yh, c: (z, 1 - yl, x, yh, c))


def to_p2(array):
    return send(array, lambda z, yl, x, yh, c: (z, 1 - yl, x, 1 - yh, c))


def to_p3(array):
    return send(array, lambda z, yl, x, yh, c: (z, yl, x, 1 - yh, c))


def shift_z(array, d):
    return send(array, lambda z, yl, x, yh, c: (z + d, yl, x, yh, c))


def shift_x(array, d):
    return send(array, lambda z, yl, x, yh, c: (z, yl, x + d, yh, c))


def silu_of_half(h):
    return h + h * jnp.tanh(h)


SMEM = pl.BlockSpec(memory_space=pltpu.SMEM)
VMEM = pl.BlockSpec(memory_space=pltpu.VMEM)


def call(kernel, scalars, arrays, outs, limit, scratch=()):
    arrays = [pltpu.with_memory_space_constraint(a, pltpu.VMEM) for a in arrays]
    return pl.pallas_call(
        kernel,
        in_specs=[SMEM] * len(scalars) + [VMEM] * len(arrays),
        out_specs=[VMEM] * len(outs),
        out_shape=[pltpu.VMEM(shape, dtype) for shape, dtype in outs],
        scratch_shapes=list(scratch),
        compiler_params=pltpu.CompilerParams(vmem_limit_bytes=limit << 20),
    )(*scalars, *arrays)


PIECE = 128


def project_rows(info, blocks, gain_ref, w_ref, put):
    gains = [gain_ref[pl.ds(info[3] ^ j, 1), :] for j in range(4)]

    def step(i, carry):
        for r in range(2):
            at = pl.ds(pl.multiple_of((2 * i + r) * PIECE, PIECE), PIECE)
            xs = [p[at, :].astype(F32) for p in blocks]
            total = sum(jnp.sum(v, axis=1, keepdims=True) for v in xs)
            mean = total * (1.0 / D)
            xs = [v - mean for v in xs]
            var = sum(jnp.sum(v * v, axis=1, keepdims=True) for v in xs) * (1.0 / D)
            inv = lax.rsqrt(var + EPS)
            acc = None
            for j, v in enumerate(xs):
                n = (v * inv * gains[j]).astype(BF)
                part = jnp.dot(n, w_ref[j * 256 : (j + 1) * 256, :], preferred_element_type=F32)
                acc = part if acc is None else acc + part
            put(at, silu_of_half(acc * 0.5).astype(BF))
        return carry

    lax.fori_loop(0, ROWS // PIECE // 2, step, 0)


def put_into(gate_ref, q_ref, kv_ref):
    def put(at, y):
        gate_ref[at, :] = y[:, :128]
        q_ref[at, :] = y[:, 256:384]
        kv_ref[at, :128] = y[:, 384:]
        kv_ref[at, 128:] = y[:, 128:256]

    return put


def other_kernel(info, *refs):
    blocks, gain_ref, w_ref = refs[:4], refs[4], refs[5]
    gate_ref, q_ref, kv_ref, w_out = refs[6:]
    for j in range(4):
        rows = pl.ds(pl.multiple_of((info[3] ^ j) * 256, 256), 256)
        for g in range(4):
            cols = pl.ds(pl.multiple_of(g * 256 + info[1] * HDIM, HDIM), HDIM)
            w_out[j * 256 : (j + 1) * 256, g * HDIM : (g + 1) * HDIM] = w_ref[rows, cols]
    project_rows(info, blocks, gain_ref, w_out, put_into(gate_ref, q_ref, kv_ref))


def own_kernel(info, *refs):
    blocks, gain_ref, w_ref, q_other = refs[:4], refs[4], refs[5], refs[6]
    gate_ref, kv_ref, q_refs, q_own = refs[7], refs[8], refs[9:13], refs[13]
    project_rows(info, blocks, gain_ref, w_ref, put_into(gate_ref, q_own, kv_ref))
    for i in range(4):
        source = (q_own, q_other)[i >> 1]
        shift = lax.rem((i ^ (2 * info[1])) - info[0] + 4, 4)
        for d in range(4):

            @pl.when(shift == d)
            def _():
                q_refs[d][...] = source[(i & 1) * SUB : ((i & 1) + 1) * SUB, :]


def project_other(info, blocks, gain, w):
    outs = [((ROWS, HDIM), BF), ((ROWS, HDIM), BF), ((ROWS, 2 * HDIM), BF), ((D, 4 * HDIM), BF)]
    return call(other_kernel, (info,), (*blocks, gain, w), outs, 8)


def project_own(info, blocks, gain, w, q_other):
    outs = [((ROWS, HDIM), BF), ((ROWS, 2 * HDIM), BF)] + [((SUB, HDIM), BF)] * 4
    scratch = [pltpu.VMEM((ROWS, HDIM), BF)]
    return call(own_kernel, (info,), (*blocks, gain, w, q_other), outs, 8, scratch)


LIST = 416


def plan_kernel(info, full_early, edge_early, full_late, edge_late):
    z, yl, x = info[0], info[1], info[2]
    far_z, far_x = lax.rem(z + 2, 4), lax.rem(x + 2, 4)

    def start_of(position):
        s = jnp.int32(0)
        for i in range(8):
            e = info[4 + i]
            s = jnp.maximum(s, jnp.where(e <= position, e, 0))
        return s

    def tiles_upto(position):
        t = position - x * ROWS
        m = lax.div(t, 4 * ROWS)
        r = lax.div(t - m * (4 * ROWS), KEYS)
        count = 3 * m + 1 + jnp.minimum(r, 2)
        return jnp.minimum(jnp.where(t < 0, 0, count), KEY_TILES)

    def list_queries(t, counts):
        first = query_first(info, t)
        begin_last = start_of(first + SUB - 1)
        low = tiles_upto(start_of(first) - KEYS)
        high = tiles_upto(first + SUB - 1)
        near = (t & 3) != far_x

        def list_keys(n, counts):
            fe, ee, fl, el = counts
            k = key_first(info, n)
            early = near & (lax.div(n, 6) != far_z)
            full = (k + KEYS - 1 <= first) & (k >= begin_last)
            entry = t * 32 + n
            full_early[fe] = entry
            edge_early[ee] = entry
            full_late[fl] = entry
            edge_late[el] = entry
            early, full = early.astype(jnp.int32), full.astype(jnp.int32)
            return (
                fe + early * full,
                ee + early * (1 - full),
                fl + (1 - early) * full,
                el + (1 - early) * (1 - full),
            )

        return lax.fori_loop(low, high, list_keys, counts)

    zero = jnp.int32(0)
    fe, ee, fl, el = lax.fori_loop(0, TILES, list_queries, (zero, zero, zero, zero))
    for fulls, nf, edges, ne in ((full_early, fe, edge_early, ee), (full_late, fl, edge_late, el)):
        groups = nf >> 2

        def move(i, ne):
            edges[ne] = fulls[i]
            return ne + 1

        ne = lax.fori_loop(groups * 4, nf, move, ne)
        edges[ne] = 512 + (z * 4 + x) * 32 + z * 6 + 3 * yl
        fulls[LIST - 1] = groups
        edges[LIST - 1] = (ne + 1) >> 1


def query_first(info, t):
    return ((t >> 2) * 8 + (info[0] >> 1) * 4 + (t & 3)) * ROWS + (info[0] & 1) * SUB


def key_first(info, n):
    m = lax.div(n, 3)
    return (m * 4 + info[2]) * ROWS + (n - 3 * m) * KEYS


def plan(info):
    return pl.pallas_call(
        plan_kernel,
        in_specs=[SMEM],
        out_specs=[SMEM] * 4,
        out_shape=[jax.ShapeDtypeStruct((LIST,), jnp.int32)] * 4,
        compiler_params=pltpu.CompilerParams(vmem_limit_bytes=1 << 20),
        name="plan",
    )(info)


def attend_kernel(info, *refs):
    lists, q_refs, kv_refs, out = refs[:4], refs[4:8], refs[8:16], refs[16]
    q, kv, acc, sem = refs[17:]
    z, yl, x = info[0], info[1], info[2]

    def load_queries(e, ref):
        copies = []
        for k in range(4):
            tile = lax.rem(z - k + 4, 4) * 4 + lax.rem(x - e + 4, 4)
            copies.append(
                pltpu.make_async_copy(
                    ref.at[pl.ds(k * SUB, SUB)],
                    q.at[pl.ds(pl.multiple_of(tile * SUB, SUB), SUB)],
                    sem.at[4 * e + k],
                )
            )
        return copies

    def load_keys(k, ref, d, rel):
        block = lax.rem(z - d + 4, 4) * 2 + (yl ^ rel)
        to = kv.at[pl.ds(pl.multiple_of(block * ROWS, ROWS), ROWS)]
        return [pltpu.make_async_copy(ref, to, sem.at[16 + k])]

    queries = [load_queries(e, ref) for e, ref in zip((0, 1, 3, 2), q_refs)]
    places = zip(kv_refs, (0, 0, 1, 1, 3, 3, 2, 2), (0, 1, 0, 1, 0, 1, 0, 1))
    keys = [load_keys(k, *place) for k, place in enumerate(places)]
    early, late = sum(keys[:6] + queries[:3], []), sum(keys[6:] + queries[3:], [])
    for c in early + late:
        c.start()
    acc[...] = jnp.zeros(acc.shape, F32)
    for c in early:
        c.wait()

    def scores(entry):
        t, n = (entry >> 5) & 15, entry & 31
        q_rows = pl.ds(pl.multiple_of(t * SUB, SUB), SUB)
        k_rows = pl.ds(pl.multiple_of(n * KEYS, KEYS), KEYS)
        s = lax.dot_general(
            q[q_rows, :], kv[k_rows, 0:HDIM], (((1,), (1,)), ((), ())), preferred_element_type=F32
        )
        return silu_of_half(s * HALF_SCALE), q_rows, k_rows, t, n

    def add(w, q_rows, k_rows):
        acc[q_rows, :] += jnp.dot(w.astype(BF), kv[k_rows, HDIM:], preferred_element_type=F32)

    def run(full_list, edge_list):
        def full_tiles(i, carry):
            for u in range(4):
                w, q_rows, k_rows, _, _ = scores(full_list[4 * i + u])
                add(w, q_rows, k_rows)
            return carry

        lax.fori_loop(0, full_list[LIST - 1], full_tiles, 0)

        def edge_tiles(i, carry):
            for u in range(2):
                entry = edge_list[2 * i + u]
                w, q_rows, k_rows, t, n = scores(entry)
                first = query_first(info, t)
                col = key_first(info, n) + lax.broadcasted_iota(jnp.int32, (1, KEYS), 1)
                ends = jnp.full((1, KEYS), FAR, jnp.int32)
                for j in range(8):
                    e = info[4 + j]
                    ends = jnp.minimum(ends, jnp.where(col < e, e, FAR))
                row = lax.broadcasted_iota(jnp.int32, (SUB, KEYS), 0)
                skip = (entry >> 9) * FAR
                allowed = (row >= col + (skip - first)) & (row < ends - first)
                add(jnp.where(allowed, w, 0.0), q_rows, k_rows)
            return carry

        lax.fori_loop(0, edge_list[LIST - 1], edge_tiles, 0)

    run(lists[0], lists[1])
    for c in late:
        c.wait()
    run(lists[2], lists[3])
    for t in range(TILES):
        out[t] = acc[t * SUB : (t + 1) * SUB, :].astype(BF)


def attend(info, lists, queries, keyvals):
    return call(
        attend_kernel,
        (info, *lists),
        (*queries, *keyvals),
        [((TILES, SUB, HDIM), BF)],
        limit=24,
        scratch=[
            pltpu.VMEM((TILES * SUB, HDIM), BF),
            pltpu.VMEM((TILES * SUB, 2 * HDIM), BF),
            pltpu.VMEM((TILES * SUB, HDIM), F32),
            pltpu.SemaphoreType.DMA((24,)),
        ],
    )[0]


def gate_kernel(info, part_ref, gate_own, gate_other, own_ref, other_ref):
    ones = jnp.ones((8, HDIM), BF)
    add_lanes = lambda v: lax.dot_general(ones, v, (((1,), (1,)), ((), ())), preferred_element_type=F32)
    for i in range(4):
        gate_ref, out, half = (gate_own, gate_other)[i >> 1], (own_ref, other_ref)[i >> 1], i & 1
        a = (i ^ (2 * info[1])) * 4
        total = part_ref[a].astype(F32)
        for b in range(1, 4):
            total = total + part_ref[a + b].astype(F32)
        at = slice(half * SUB, (half + 1) * SUB)
        out[at, :] = (total * gate_ref[at, :].astype(F32)).astype(BF)
        square = total * total
        top = square.astype(BF)
        sums = add_lanes(top) + add_lanes((square - top.astype(F32)).astype(BF))
        for c in range(SUB // HDIM):
            value = sums[:, c * HDIM : (c + 1) * HDIM]
            top = value.astype(BF)
            to = ROWS + TAIL * (3 * half + c)
            out[to : to + 8, :] = top
            out[to + 8 : to + 16, :] = (value - top.astype(F32)).astype(BF)


def gate_rows(info, parts, gate_own, gate_other):
    outs = [((ROWS + 6 * TAIL, HDIM), BF)] * 2
    return call(gate_kernel, (info,), (parts, gate_own, gate_other), outs, 8)


def mix_kernel(info, *refs):
    rows, w_here, w_there = refs[:4], refs[4], refs[5]
    mine_ref, theirs_ref, squares_ref = refs[6:]
    core = info[3] & 1
    for out, c in ((theirs_ref, 1 - core), (mine_ref, core)):
        cols = pl.ds(pl.multiple_of(c * 256, 256), 256)
        acc = None
        for r, w, flip in zip(rows, (w_here, w_here, w_there, w_there), (0, 1, 1, 0)):
            at = pl.ds(pl.multiple_of((info[1] ^ flip) * HDIM, HDIM), HDIM)
            part = jnp.dot(r[0:ROWS, :], w[at, cols], preferred_element_type=F32)
            acc = part if acc is None else acc + part
        out[0:ROWS, :] = acc
    tail = sum(r[ROWS:, :].astype(F32) for r in rows)
    lines = [tail[TAIL * c : TAIL * c + 1] + tail[TAIL * c + 8 : TAIL * c + 9] for c in range(6)]
    squares = jnp.concatenate(lines + [jnp.zeros((2, HDIM), F32)], axis=0)
    squares_ref[...] = squares
    theirs_ref[ROWS:, 0:HDIM] = squares
    theirs_ref[ROWS:, HDIM:] = squares


def mix(info, gated, w_here, w_there):
    outs = [((ROWS, 256), F32), ((ROWS + 8, 256), F32), ((8, HDIM), F32)]
    return call(mix_kernel, (info,), (*gated, w_here, w_there), outs, 12)


def finish_kernel(mine_ref, got_ref, squares_ref, ev_ref, out_ref, rows, sem):
    inv = lax.rsqrt((squares_ref[...] + got_ref[ROWS:, 0:HDIM]) * (1.0 / D) + EPS)
    eye = lax.broadcasted_iota(jnp.int32, (HDIM, HDIM), 0) == lax.broadcasted_iota(jnp.int32, (HDIM, HDIM), 1)
    copies = []
    for k in range(6):
        column = jnp.sum(jnp.where(eye, inv[k : k + 1, :], 0.0), axis=1, keepdims=True)
        at = slice(k * HDIM, (k + 1) * HDIM)
        total = mine_ref[at, :] + got_ref[at, :]
        rows[at, :] = (ev_ref[at, :].astype(F32) + total * column).astype(BF)
        copies.append(pltpu.make_async_copy(rows.at[at], out_ref.at[at], sem.at[k]))
        copies[-1].start()
    for c in copies:
        c.wait()


def finish(mine, got, squares, events):
    arrays = [pltpu.with_memory_space_constraint(a, pltpu.VMEM) for a in (mine, got, squares, events)]
    return pl.pallas_call(
        finish_kernel,
        in_specs=[VMEM] * 4,
        out_specs=pl.BlockSpec(memory_space=pl.ANY),
        out_shape=jax.ShapeDtypeStruct((ROWS, 256), BF),
        scratch_shapes=[pltpu.VMEM((ROWS, 256), BF), pltpu.SemaphoreType.DMA((6,))],
        compiler_params=pltpu.CompilerParams(vmem_limit_bytes=8 << 20),
        name="finish",
    )(*arrays)


def layer(events, norm_gain, w_uvqk, w_out, lengths):
    z, yl, x = (lax.axis_index(a).astype(jnp.int32) for a in ("z", "yl", "x"))
    yh = lax.axis_index("yh").astype(jnp.int32)
    o = yh * 2 + lax.axis_index("core").astype(jnp.int32)
    info = jnp.concatenate([jnp.stack([z, yl, x, o]), jnp.cumsum(lengths).astype(jnp.int32)])

    p1, p2, p3 = to_p1(events), to_p2(events), to_p3(events)
    c0 = flip_core(events)
    w_in = w_uvqk.reshape(D, 4 * 256)
    gain = norm_gain.reshape(4, 256)
    p1, w_in, info, gain = lax.optimization_barrier((p1, w_in, info, gain))
    c1, c2, c3 = flip_core(p1), flip_core(p2), flip_core(p3)

    gate_other, q_other, kv_other, w_in = project_other(info, (p1, c1, p2, c2), gain, w_in)
    gate_own, kv_own, *pieces = project_own(info, (events, c0, p3, c3), gain, w_in, q_other)

    pieces = [pieces[0]] + [shift_z(pieces[d], d) for d in (1, 2, 3)]
    up_other, down_other = shift_z(kv_other, 1), shift_z(kv_other, -1)
    up_own, down_own = shift_z(kv_own, 1), shift_z(kv_own, -1)

    q_mine = jnp.concatenate(pieces, axis=0)
    queries = [q_mine] + [shift_x(q_mine, e) for e in (1, 3, 2)]
    near, away = shift_z(up_own, 1), shift_z(down_other, -1)

    keyvals = [kv_own, kv_other, up_own, up_other, down_own, down_other, near, away]
    lists = plan(info)
    parts = attend(info, lists, queries, keyvals)

    w_here = lax.dynamic_slice_in_dim(w_out, yh * 512, 512, 1)
    w_away = lax.dynamic_slice_in_dim(w_out, (1 - yh) * 512, 512, 1)
    w_away, _ = lax.optimization_barrier((w_away, q_mine))
    w_there = to_p3(w_away)

    parts = lax.all_to_all(parts, ("z", "x"), 0, 0)
    own, other = gate_rows(info, parts, gate_own, gate_other)
    gated = [own, to_p1(other), to_p2(other), to_p3(own)]
    mine, theirs, squares = mix(info, gated, w_here, w_there)
    return finish(mine, flip_core(theirs), squares, events)


def solution(mesh):
    fine = Mesh(mesh.devices.reshape(SIZES), AXES)
    ctx, head = ("z", "yl", "x"), ("yh", "core")
    in_specs = (P(ctx, head), P(), P(None, None, head), P(head, None), P())
    return jax.shard_map(layer, mesh=fine, in_specs=in_specs, out_specs=P(ctx, head), check_vma=False)
```

```python
import jax
import jax.numpy as jnp
import numpy as np
from jax import lax
from jax.experimental import pallas as pl
from jax.experimental.pallas import tpu as pltpu
from jax.sharding import Mesh
from jax.sharding import PartitionSpec as P


D = 1024
HDIM = 128
ROWS = 768
SUB = 384
TILES = 16
KEYS = 256
KEY_TILES = 24
TAIL = 16
EPS = 1e-05
AXES = ("z", "yl", "x", "yh", "core")
SIZES = (4, 2, 4, 2, 2)
HALF_SCALE = 0.5 * HDIM ** (-0.5)
FAR = 1 << 24
BF = jnp.bfloat16
F32 = jnp.float32


def send(array, target):
    pairs = []
    for source in range(int(np.prod(SIZES))):
        place = np.unravel_index(source, SIZES)
        dest = [int(t) % n for t, n in zip(target(*[int(p) for p in place]), SIZES)]
        pairs.append((source, int(np.ravel_multi_index(dest, SIZES))))
    return lax.ppermute(array, AXES, pairs)


def flip_core(array):
    return send(array, lambda z, yl, x, yh, c: (z, yl, x, yh, 1 - c))


def to_p1(array):
    return send(array, lambda z, yl, x, yh, c: (z, 1 - yl, x, yh, c))


def to_p2(array):
    return send(array, lambda z, yl, x, yh, c: (z, 1 - yl, x, 1 - yh, c))


def to_p3(array):
    return send(array, lambda z, yl, x, yh, c: (z, yl, x, 1 - yh, c))


def shift_z(array, d):
    return send(array, lambda z, yl, x, yh, c: (z + d, yl, x, yh, c))


def shift_x(array, d):
    return send(array, lambda z, yl, x, yh, c: (z, yl, x + d, yh, c))


def silu_of_half(h):
    return h + h * jnp.tanh(h)


SMEM = pl.BlockSpec(memory_space=pltpu.SMEM)
VMEM = pl.BlockSpec(memory_space=pltpu.VMEM)


def call(kernel, scalars, arrays, outs, limit, scratch=(), aliases={}):
    arrays = [pltpu.with_memory_space_constraint(a, pltpu.VMEM) for a in arrays]
    return pl.pallas_call(
        kernel,
        in_specs=[SMEM] * len(scalars) + [VMEM] * len(arrays),
        out_specs=[VMEM] * len(outs),
        out_shape=[pltpu.VMEM(shape, dtype) for shape, dtype in outs],
        scratch_shapes=list(scratch),
        input_output_aliases=aliases,
        compiler_params=pltpu.CompilerParams(vmem_limit_bytes=limit << 20),
    )(*scalars, *arrays)


PIECE = 128
PER = 3


def project_rows(info, blocks, gain_ref, w_ref, put, offset=0, rows=ROWS):
    gains = [gain_ref[pl.ds(info[3] ^ j, 1), :] for j in range(4)]

    def step(i, carry):
        for r in range(PER):
            here = (PER * i + r) * PIECE + offset
            at = pl.ds(pl.multiple_of(here, PIECE), PIECE)
            xs = [p[pl.ds(pl.multiple_of(here - f, PIECE), PIECE), :].astype(F32) for p, f in blocks]
            total = sum(jnp.sum(v, axis=1, keepdims=True) for v in xs)
            mean = total * (1.0 / D)
            xs = [v - mean for v in xs]
            var = sum(jnp.sum(v * v, axis=1, keepdims=True) for v in xs) * (1.0 / D)
            inv = lax.rsqrt(var + EPS)
            acc = None
            for j, v in enumerate(xs):
                n = (v * inv * gains[j]).astype(BF)
                part = jnp.dot(n, w_ref[j * 256 : (j + 1) * 256, :], preferred_element_type=F32)
                acc = part if acc is None else acc + part
            put(at, silu_of_half(acc * 0.5).astype(BF))
        return carry

    lax.fori_loop(0, rows // PIECE // PER, step, 0)


def put_into(gate_ref, q_ref, kv_ref):
    def put(at, y):
        gate_ref[at, :] = y[:, :128]
        q_ref[at, :] = y[:, 256:384]
        kv_ref[at, :128] = y[:, 384:]
        kv_ref[at, 128:] = y[:, 128:256]

    return put


def other_kernel(info, *refs):
    blocks, gain_ref, w_ref = refs[:4], refs[4], refs[5]
    gate_ref, q_ref, kv_ref, w_out = refs[6:]
    for j in range(4):
        rows = pl.ds(pl.multiple_of((info[3] ^ j) * 256, 256), 256)
        for g in range(4):
            cols = pl.ds(pl.multiple_of(g * 256 + info[1] * HDIM, HDIM), HDIM)
            w_out[j * 256 : (j + 1) * 256, g * HDIM : (g + 1) * HDIM] = w_ref[rows, cols]
    project_rows(info, [(b, 0) for b in blocks], gain_ref, w_out, put_into(gate_ref, q_ref, kv_ref))


def own_kernel(info, *refs):
    here, core, far, far_core = refs[0], refs[1], refs[2:4], refs[4:6]
    gain_ref, w_ref, q_other = refs[6:9]
    gate_ref, kv_ref, q_refs, q_own = refs[9], refs[10], refs[11:15], refs[15]
    put = put_into(gate_ref, q_own, kv_ref)
    for half in range(2):
        at = half * SUB
        blocks = [(here, 0), (core, 0), (far[half], at), (far_core[half], at)]
        project_rows(info, blocks, gain_ref, w_ref, put, at, SUB)
    for i in range(4):
        source = (q_own, q_other)[i >> 1]
        shift = lax.rem((i ^ (2 * info[1])) - info[0] + 4, 4)
        for d in range(4):

            @pl.when(shift == d)
            def _():
                q_refs[d][...] = source[(i & 1) * SUB : ((i & 1) + 1) * SUB, :]


def project_other(info, blocks, gain, w):
    outs = [((ROWS, HDIM), BF), ((ROWS, HDIM), BF), ((ROWS, 2 * HDIM), BF), ((D, 4 * HDIM), BF)]
    return call(other_kernel, (info,), (*blocks, gain, w), outs, 8)


def project_own(info, blocks, gain, w, q_other):
    outs = [((ROWS, HDIM), BF), ((ROWS, 2 * HDIM), BF)] + [((SUB, HDIM), BF)] * 4
    scratch = [pltpu.VMEM((ROWS, HDIM), BF)]
    return call(own_kernel, (info,), (*blocks, gain, w, q_other), outs, 8, scratch)


LIST = 416


def plan_kernel(info, full_early, edge_early, full_late, edge_late):
    z, yl, x = info[0], info[1], info[2]
    far_z, far_x = lax.rem(z + 2, 4), lax.rem(x + 2, 4)

    def start_of(position):
        s = jnp.int32(0)
        for i in range(8):
            e = info[4 + i]
            s = jnp.maximum(s, jnp.where(e <= position, e, 0))
        return s

    def tiles_upto(position):
        t = position - x * ROWS
        m = lax.div(t, 4 * ROWS)
        r = lax.div(t - m * (4 * ROWS), KEYS)
        count = 3 * m + 1 + jnp.minimum(r, 2)
        return jnp.minimum(jnp.where(t < 0, 0, count), KEY_TILES)

    def list_queries(t, counts):
        first = query_first(info, t)
        begin_last = start_of(first + SUB - 1)
        low = tiles_upto(start_of(first) - KEYS)
        high = tiles_upto(first + SUB - 1)
        near = (t & 3) != far_x

        def list_keys(n, counts):
            fe, ee, fl, el = counts
            k = key_first(info, n)
            early = near & (lax.div(n, 6) != far_z)
            full = (k + KEYS - 1 <= first) & (k >= begin_last)
            entry = t * 32 + n
            full_early[fe] = entry
            edge_early[ee] = entry
            full_late[fl] = entry
            edge_late[el] = entry
            early, full = early.astype(jnp.int32), full.astype(jnp.int32)
            return (
                fe + early * full,
                ee + early * (1 - full),
                fl + (1 - early) * full,
                el + (1 - early) * (1 - full),
            )

        return lax.fori_loop(low, high, list_keys, counts)

    zero = jnp.int32(0)
    fe, ee, fl, el = lax.fori_loop(0, TILES, list_queries, (zero, zero, zero, zero))
    for fulls, nf, edges, ne in ((full_early, fe, edge_early, ee), (full_late, fl, edge_late, el)):
        groups = nf >> 2

        def move(i, ne):
            edges[ne] = fulls[i]
            return ne + 1

        ne = lax.fori_loop(groups * 4, nf, move, ne)
        edges[ne] = 512 + (z * 4 + x) * 32 + z * 6 + 3 * yl
        fulls[LIST - 1] = groups
        edges[LIST - 1] = (ne + 1) >> 1


def query_first(info, t):
    return ((t >> 2) * 8 + (info[0] >> 1) * 4 + (t & 3)) * ROWS + (info[0] & 1) * SUB


def key_first(info, n):
    m = lax.div(n, 3)
    return (m * 4 + info[2]) * ROWS + (n - 3 * m) * KEYS


def plan(info):
    return pl.pallas_call(
        plan_kernel,
        in_specs=[SMEM],
        out_specs=[SMEM] * 4,
        out_shape=[jax.ShapeDtypeStruct((LIST,), jnp.int32)] * 4,
        compiler_params=pltpu.CompilerParams(vmem_limit_bytes=1 << 20),
        name="plan",
    )(info)


def load_queries(info, e, ref, q, sem):
    z, x = info[0], info[2]
    copies = []
    for k in range(4):
        tile = lax.rem(z - k + 4, 4) * 4 + lax.rem(x - e + 4, 4)
        to = q.at[pl.ds(pl.multiple_of(tile * SUB, SUB), SUB)]
        copies.append(pltpu.make_async_copy(ref.at[pl.ds(k * SUB, SUB)], to, sem.at[4 * e + k]))
    return copies


def load_keys(info, d, rel, ref, kv, sem):
    block = lax.rem(info[0] - d + 4, 4) * 2 + (info[1] ^ rel)
    to = kv.at[pl.ds(pl.multiple_of(block * ROWS, ROWS), ROWS)]
    return [pltpu.make_async_copy(ref, to, sem.at[16 + 2 * d + rel])]


def add_tiles(info, full_list, edge_list, q, kv, acc):
    def scores(entry):
        t, n = (entry >> 5) & 15, entry & 31
        q_rows = pl.ds(pl.multiple_of(t * SUB, SUB), SUB)
        k_rows = pl.ds(pl.multiple_of(n * KEYS, KEYS), KEYS)
        s = lax.dot_general(
            q[q_rows, :], kv[k_rows, 0:HDIM], (((1,), (1,)), ((), ())), preferred_element_type=F32
        )
        return silu_of_half(s * HALF_SCALE), q_rows, k_rows, t, n

    def add(w, q_rows, k_rows):
        acc[q_rows, :] += jnp.dot(w.astype(BF), kv[k_rows, HDIM:], preferred_element_type=F32)

    def full_tiles(i, carry):
        for u in range(4):
            w, q_rows, k_rows, _, _ = scores(full_list[4 * i + u])
            add(w, q_rows, k_rows)
        return carry

    lax.fori_loop(0, full_list[LIST - 1], full_tiles, 0)

    def edge_tiles(i, carry):
        for u in range(2):
            entry = edge_list[2 * i + u]
            w, q_rows, k_rows, t, n = scores(entry)
            first = query_first(info, t)
            col = key_first(info, n) + lax.broadcasted_iota(jnp.int32, (1, KEYS), 1)
            ends = jnp.full((1, KEYS), FAR, jnp.int32)
            for j in range(8):
                e = info[4 + j]
                ends = jnp.minimum(ends, jnp.where(col < e, e, FAR))
            row = lax.broadcasted_iota(jnp.int32, (SUB, KEYS), 0)
            skip = (entry >> 9) * FAR
            allowed = (row >= col + (skip - first)) & (row < ends - first)
            add(jnp.where(allowed, w, 0.0), q_rows, k_rows)
        return carry

    lax.fori_loop(0, edge_list[LIST - 1], edge_tiles, 0)


def early_kernel(info, full_list, edge_list, *refs):
    q_refs, kv_refs = refs[:3], refs[3:9]
    acc, q, kv, sem = refs[9:]
    copies = sum([load_queries(info, e, ref, q, sem) for e, ref in zip((0, 1, 3), q_refs)], [])
    for i, ref in enumerate(kv_refs):
        copies += load_keys(info, (0, 1, 3)[i >> 1], i & 1, ref, kv, sem)
    for c in copies:
        c.start()
    acc[...] = jnp.zeros(acc.shape, F32)
    for c in copies:
        c.wait()
    add_tiles(info, full_list, edge_list, q, kv, acc)


HELD = (((TILES * SUB, HDIM), F32), ((TILES * SUB, HDIM), BF), ((TILES * SUB, 2 * HDIM), BF))


def attend_early(info, lists, queries, keyvals):
    scratch = [pltpu.SemaphoreType.DMA((24,))]
    return call(early_kernel, (info, *lists), (*queries, *keyvals), HELD, 4, scratch)


def late_kernel(info, full_list, edge_list, acc_in, q_in, kv_in, far_q, near, away, out, acc, q, kv, sem):
    copies = load_queries(info, 2, far_q, q, sem)
    copies += load_keys(info, 2, 0, near, kv, sem) + load_keys(info, 2, 1, away, kv, sem)
    for c in copies:
        c.start()
    for c in copies:
        c.wait()
    add_tiles(info, full_list, edge_list, q, kv, acc)
    for t in range(TILES):
        out[t] = acc[t * SUB : (t + 1) * SUB, :].astype(BF)


def attend_late(info, lists, held, far_q, near, away):
    scratch = [pltpu.SemaphoreType.DMA((24,))]
    outs = (((TILES, SUB, HDIM), BF), *HELD)
    aliases = {3: 1, 4: 2, 5: 3}
    return call(late_kernel, (info, *lists), (*held, far_q, near, away), outs, 4, scratch, aliases)[0]


def gate_kernel(info, part_ref, gate_own, gate_other, own_ref, other_ref):
    ones = jnp.ones((8, HDIM), BF)
    add_lanes = lambda v: lax.dot_general(ones, v, (((1,), (1,)), ((), ())), preferred_element_type=F32)
    for gate_ref, out, rel in ((gate_own, own_ref, 0), (gate_other, other_ref, 1)):
        high, low = [], []
        for half in range(2):
            a = ((2 * rel + half) ^ (2 * info[1])) * 4
            total = part_ref[a].astype(F32)
            for b in range(1, 4):
                total = total + part_ref[a + b].astype(F32)
            at = slice(half * SUB, (half + 1) * SUB)
            out[at, :] = (total * gate_ref[at, :].astype(F32)).astype(BF)
            square = total * total
            top = square.astype(BF)
            sums = add_lanes(top) + add_lanes((square - top.astype(F32)).astype(BF))
            for c in range(SUB // HDIM):
                value = sums[0:1, c * HDIM : (c + 1) * HDIM]
                top = value.astype(BF).astype(F32)
                high.append(top)
                low.append(value - top)
        out[ROWS:, :] = jnp.concatenate(high + low + [jnp.zeros((4, HDIM), F32)], axis=0).astype(BF)


def gate_rows(info, parts, gate_own, gate_other):
    outs = [((ROWS + TAIL, HDIM), BF)] * 2
    return call(gate_kernel, (info,), (parts, gate_own, gate_other), outs, 8)


def mix_kernel(info, *refs):
    rows, w_here, w_there = refs[:4], refs[4], refs[5]
    mine_ref, theirs_ref, squares_ref = refs[6:]
    core = info[3] & 1
    for out, c in ((theirs_ref, 1 - core), (mine_ref, core)):
        cols = pl.ds(pl.multiple_of(c * 256, 256), 256)
        acc = None
        for r, w, flip in zip(rows, (w_here, w_here, w_there, w_there), (0, 1, 1, 0)):
            at = pl.ds(pl.multiple_of((info[1] ^ flip) * HDIM, HDIM), HDIM)
            part = jnp.dot(r[0:ROWS, :], w[at, cols], preferred_element_type=F32)
            acc = part if acc is None else acc + part
        out[0:ROWS, :] = acc
    tail = sum(r[ROWS:, :].astype(F32) for r in rows)
    squares = jnp.concatenate([tail[0:6] + tail[6:12], jnp.zeros((2, HDIM), F32)], axis=0)
    squares_ref[...] = squares
    theirs_ref[ROWS:, 0:HDIM] = squares
    theirs_ref[ROWS:, HDIM:] = squares


def mix(info, gated, w_here, w_there):
    outs = [((ROWS, 256), F32), ((ROWS + 8, 256), F32), ((8, HDIM), F32)]
    return call(mix_kernel, (info,), (*gated, w_here, w_there), outs, 12)


def finish_kernel(mine_ref, got_ref, squares_ref, ev_ref, out_ref, rows, sem):
    inv = lax.rsqrt((squares_ref[...] + got_ref[ROWS:, 0:HDIM]) * (1.0 / D) + EPS)
    eye = lax.broadcasted_iota(jnp.int32, (HDIM, HDIM), 0) == lax.broadcasted_iota(jnp.int32, (HDIM, HDIM), 1)
    copies = []
    for k in range(6):
        column = jnp.sum(jnp.where(eye, inv[k : k + 1, :], 0.0), axis=1, keepdims=True)
        at = slice(k * HDIM, (k + 1) * HDIM)
        total = mine_ref[at, :] + got_ref[at, :]
        rows[at, :] = (ev_ref[at, :].astype(F32) + total * column).astype(BF)
        copies.append(pltpu.make_async_copy(rows.at[at], out_ref.at[at], sem.at[k]))
        copies[-1].start()
    for c in copies:
        c.wait()


def finish(mine, got, squares, events):
    arrays = [pltpu.with_memory_space_constraint(a, pltpu.VMEM) for a in (mine, got, squares, events)]
    return pl.pallas_call(
        finish_kernel,
        in_specs=[VMEM] * 4,
        out_specs=pl.BlockSpec(memory_space=pl.ANY),
        out_shape=jax.ShapeDtypeStruct((ROWS, 256), BF),
        scratch_shapes=[pltpu.VMEM((ROWS, 256), BF), pltpu.SemaphoreType.DMA((6,))],
        compiler_params=pltpu.CompilerParams(vmem_limit_bytes=8 << 20),
        name="finish",
    )(*arrays)


def layer(events, norm_gain, w_uvqk, w_out, lengths):
    z, yl, x = (lax.axis_index(a).astype(jnp.int32) for a in ("z", "yl", "x"))
    yh = lax.axis_index("yh").astype(jnp.int32)
    o = yh * 2 + lax.axis_index("core").astype(jnp.int32)
    info = jnp.concatenate([jnp.stack([z, yl, x, o]), jnp.cumsum(lengths).astype(jnp.int32)])

    p1, p2 = to_p1(events), to_p2(events)
    c0 = flip_core(events)
    w_in = w_uvqk.reshape(D, 4 * 256)
    gain = norm_gain.reshape(4, 256)
    p1, w_in, info, gain = lax.optimization_barrier((p1, w_in, info, gain))
    far = [to_p2(p1[:SUB]), to_p1(p2[SUB:])]
    c1, c2 = flip_core(p1), flip_core(p2)
    far_core = [flip_core(far[0]), flip_core(far[1])]

    gate_other, q_other, kv_other, w_in = project_other(info, (p1, c1, p2, c2), gain, w_in)
    gate_own, kv_own, *pieces = project_own(info, (events, c0, *far, *far_core), gain, w_in, q_other)

    pieces = [pieces[0]] + [shift_z(pieces[d], d) for d in (1, 2, 3)]
    up_other, down_other = shift_z(kv_other, 1), shift_z(kv_other, -1)
    up_own, down_own = shift_z(kv_own, 1), shift_z(kv_own, -1)

    q_mine = jnp.concatenate(pieces, axis=0)
    queries = [q_mine] + [shift_x(q_mine, e) for e in (1, 3, 2)]
    near, away = shift_z(up_own, 1), shift_z(down_other, -1)

    keyvals = [kv_own, kv_other, up_own, up_other, down_own, down_other]
    lists = plan(info)
    held = attend_early(info, lists[:2], queries[:3], keyvals)
    parts = attend_late(info, lists[2:], held, queries[3], near, away)

    w_here = lax.dynamic_slice_in_dim(w_out, yh * 512, 512, 1)
    w_away = lax.dynamic_slice_in_dim(w_out, (1 - yh) * 512, 512, 1)
    w_away, _ = lax.optimization_barrier((w_away, q_mine))
    w_there = to_p3(w_away)

    parts = lax.all_to_all(parts, ("z", "x"), 0, 0)
    own, other = gate_rows(info, parts, gate_own, gate_other)
    gated = [own, to_p1(other), to_p2(other), to_p3(own)]
    mine, theirs, squares = mix(info, gated, w_here, w_there)
    return finish(mine, flip_core(theirs), squares, events)


def solution(mesh):
    fine = Mesh(mesh.devices.reshape(SIZES), AXES)
    ctx, head = ("z", "yl", "x"), ("yh", "core")
    in_specs = (P(ctx, head), P(), P(None, None, head), P(head, None), P())
    return jax.shard_map(layer, mesh=fine, in_specs=in_specs, out_specs=P(ctx, head), check_vma=False)
```

```python
import jax
import jax.numpy as jnp
import numpy as np
from jax import lax
from jax.experimental import pallas as pl
from jax.experimental.pallas import tpu as pltpu
from jax.sharding import Mesh
from jax.sharding import PartitionSpec as P


D = 1024
HDIM = 128
ROWS = 768
SUB = 384
TILES = 16
KEYS = 256
KEY_TILES = 24
TAIL = 16
EPS = 1e-05
AXES = ("z", "yl", "x", "yh", "core")
SIZES = (4, 2, 4, 2, 2)
HALF_SCALE = 0.5 * HDIM ** (-0.5)
FAR = 1 << 24
BF = jnp.bfloat16
F32 = jnp.float32


def send(array, target):
    pairs = []
    for source in range(int(np.prod(SIZES))):
        place = np.unravel_index(source, SIZES)
        dest = [int(t) % n for t, n in zip(target(*[int(p) for p in place]), SIZES)]
        pairs.append((source, int(np.ravel_multi_index(dest, SIZES))))
    return lax.ppermute(array, AXES, pairs)


def flip_core(array):
    return send(array, lambda z, yl, x, yh, c: (z, yl, x, yh, 1 - c))


def to_p1(array):
    return send(array, lambda z, yl, x, yh, c: (z, 1 - yl, x, yh, c))


def to_p2(array):
    return send(array, lambda z, yl, x, yh, c: (z, 1 - yl, x, 1 - yh, c))


def to_p3(array):
    return send(array, lambda z, yl, x, yh, c: (z, yl, x, 1 - yh, c))


def shift_z(array, d):
    return send(array, lambda z, yl, x, yh, c: (z + d, yl, x, yh, c))


def shift_x(array, d):
    return send(array, lambda z, yl, x, yh, c: (z, yl, x + d, yh, c))


def silu_of_half(h):
    return h + h * jnp.tanh(h)


SMEM = pl.BlockSpec(memory_space=pltpu.SMEM)
VMEM = pl.BlockSpec(memory_space=pltpu.VMEM)


def call(kernel, scalars, arrays, outs, limit, scratch=(), aliases={}):
    arrays = [pltpu.with_memory_space_constraint(a, pltpu.VMEM) for a in arrays]
    return pl.pallas_call(
        kernel,
        in_specs=[SMEM] * len(scalars) + [VMEM] * len(arrays),
        out_specs=[VMEM] * len(outs),
        out_shape=[pltpu.VMEM(shape, dtype) for shape, dtype in outs],
        scratch_shapes=list(scratch),
        input_output_aliases=aliases,
        compiler_params=pltpu.CompilerParams(vmem_limit_bytes=limit << 20),
    )(*scalars, *arrays)


PIECE = 128
PER = 3


def project_rows(info, blocks, gain_ref, w_ref, put, offset=0, rows=ROWS):
    gains = [gain_ref[pl.ds(info[3] ^ j, 1), :] for j in range(4)]

    def step(i, carry):
        for r in range(PER):
            here = (PER * i + r) * PIECE + offset
            at = pl.ds(pl.multiple_of(here, PIECE), PIECE)
            xs = [p[pl.ds(pl.multiple_of(here - f, PIECE), PIECE), :].astype(F32) for p, f in blocks]
            total = sum(jnp.sum(v, axis=1, keepdims=True) for v in xs)
            mean = total * (1.0 / D)
            xs = [v - mean for v in xs]
            var = sum(jnp.sum(v * v, axis=1, keepdims=True) for v in xs) * (1.0 / D)
            inv = lax.rsqrt(var + EPS)
            acc = None
            for j, v in enumerate(xs):
                n = (v * inv * gains[j]).astype(BF)
                part = jnp.dot(n, w_ref[j * 256 : (j + 1) * 256, :], preferred_element_type=F32)
                acc = part if acc is None else acc + part
            put(at, silu_of_half(acc * 0.5).astype(BF))
        return carry

    lax.fori_loop(0, rows // PIECE // PER, step, 0)


def put_into(gate_ref, q_ref, kv_ref):
    def put(at, y):
        gate_ref[at, :] = y[:, :128]
        q_ref[at, :] = y[:, 256:384]
        kv_ref[at, :128] = y[:, 384:]
        kv_ref[at, 128:] = y[:, 128:256]

    return put


def other_kernel(info, *refs):
    blocks, gain_ref, w_ref = refs[:4], refs[4], refs[5]
    gate_ref, q_ref, kv_ref, w_out = refs[6:]
    for j in range(4):
        rows = pl.ds(pl.multiple_of((info[3] ^ j) * 256, 256), 256)
        for g in range(4):
            cols = pl.ds(pl.multiple_of(g * 256 + info[1] * HDIM, HDIM), HDIM)
            w_out[j * 256 : (j + 1) * 256, g * HDIM : (g + 1) * HDIM] = w_ref[rows, cols]
    project_rows(info, [(b, 0) for b in blocks], gain_ref, w_out, put_into(gate_ref, q_ref, kv_ref))


def own_kernel(info, *refs):
    here, core, far, far_core = refs[0], refs[1], refs[2:4], refs[4:6]
    gain_ref, w_ref, q_other = refs[6:9]
    gate_ref, kv_ref, q_refs, q_own = refs[9], refs[10], refs[11:15], refs[15]
    put = put_into(gate_ref, q_own, kv_ref)
    for half in range(2):
        at = half * SUB
        blocks = [(here, 0), (core, 0), (far[half], at), (far_core[half], at)]
        project_rows(info, blocks, gain_ref, w_ref, put, at, SUB)
    for i in range(4):
        source = (q_own, q_other)[i >> 1]
        shift = lax.rem((i ^ (2 * info[1])) - info[0] + 4, 4)
        for d in range(4):

            @pl.when(shift == d)
            def _():
                q_refs[d][...] = source[(i & 1) * SUB : ((i & 1) + 1) * SUB, :]


def project_other(info, blocks, gain, w):
    outs = [((ROWS, HDIM), BF), ((ROWS, HDIM), BF), ((ROWS, 2 * HDIM), BF), ((D, 4 * HDIM), BF)]
    return call(other_kernel, (info,), (*blocks, gain, w), outs, 8)


def project_own(info, blocks, gain, w, q_other):
    outs = [((ROWS, HDIM), BF), ((ROWS, 2 * HDIM), BF)] + [((SUB, HDIM), BF)] * 4
    scratch = [pltpu.VMEM((ROWS, HDIM), BF)]
    return call(own_kernel, (info,), (*blocks, gain, w, q_other), outs, 8, scratch)


LIST = 416


def plan_kernel(info, full_early, edge_early, full_late, edge_late):
    z, yl, x = info[0], info[1], info[2]
    far_z, far_x = lax.rem(z + 2, 4), lax.rem(x + 2, 4)

    def start_of(position):
        s = jnp.int32(0)
        for i in range(8):
            e = info[4 + i]
            s = jnp.maximum(s, jnp.where(e <= position, e, 0))
        return s

    def tiles_upto(position):
        t = position - x * ROWS
        m = lax.div(t, 4 * ROWS)
        r = lax.div(t - m * (4 * ROWS), KEYS)
        count = 3 * m + 1 + jnp.minimum(r, 2)
        return jnp.minimum(jnp.where(t < 0, 0, count), KEY_TILES)

    def list_queries(t, counts):
        first = query_first(info, t)
        begin_last = start_of(first + SUB - 1)
        low = tiles_upto(start_of(first) - KEYS)
        high = tiles_upto(first + SUB - 1)
        near = (t & 3) != far_x

        def list_keys(n, counts):
            fe, ee, fl, el = counts
            k = key_first(info, n)
            early = near & (lax.div(n, 6) != far_z)
            full = (k + KEYS - 1 <= first) & (k >= begin_last)
            entry = t * 32 + n
            full_early[fe] = entry
            edge_early[ee] = entry
            full_late[fl] = entry
            edge_late[el] = entry
            early, full = early.astype(jnp.int32), full.astype(jnp.int32)
            return (
                fe + early * full,
                ee + early * (1 - full),
                fl + (1 - early) * full,
                el + (1 - early) * (1 - full),
            )

        return lax.fori_loop(low, high, list_keys, counts)

    zero = jnp.int32(0)
    fe, ee, fl, el = lax.fori_loop(0, TILES, list_queries, (zero, zero, zero, zero))
    for fulls, nf, edges, ne in ((full_early, fe, edge_early, ee), (full_late, fl, edge_late, el)):
        groups = nf >> 2

        def move(i, ne):
            edges[ne] = fulls[i]
            return ne + 1

        ne = lax.fori_loop(groups * 4, nf, move, ne)
        edges[ne] = 512 + (z * 4 + x) * 32 + z * 6 + 3 * yl
        fulls[LIST - 1] = groups
        edges[LIST - 1] = (ne + 1) >> 1


def query_first(info, t):
    return ((t >> 2) * 8 + (info[0] >> 1) * 4 + (t & 3)) * ROWS + (info[0] & 1) * SUB


def key_first(info, n):
    m = lax.div(n, 3)
    return (m * 4 + info[2]) * ROWS + (n - 3 * m) * KEYS


def plan(info):
    return pl.pallas_call(
        plan_kernel,
        in_specs=[SMEM],
        out_specs=[SMEM] * 4,
        out_shape=[jax.ShapeDtypeStruct((LIST,), jnp.int32)] * 4,
        compiler_params=pltpu.CompilerParams(vmem_limit_bytes=1 << 20),
        name="plan",
    )(info)


def place_queries(info, e, ref, q):
    for k in range(4):
        tile = lax.rem(info[0] - k + 4, 4) * 4 + lax.rem(info[2] - e + 4, 4)
        q[pl.ds(pl.multiple_of(tile * SUB, SUB), SUB), :] = ref[k * SUB : (k + 1) * SUB, :]


def place_keys(info, d, rel, ref, kv):
    block = lax.rem(info[0] - d + 4, 4) * 2 + (info[1] ^ rel)
    kv[pl.ds(pl.multiple_of(block * ROWS, ROWS), ROWS), :] = ref[...]


def add_tiles(info, full_list, edge_list, q, kv, acc):
    def scores(entry):
        t, n = (entry >> 5) & 15, entry & 31
        q_rows = pl.ds(pl.multiple_of(t * SUB, SUB), SUB)
        k_rows = pl.ds(pl.multiple_of(n * KEYS, KEYS), KEYS)
        s = lax.dot_general(
            q[q_rows, :], kv[k_rows, 0:HDIM], (((1,), (1,)), ((), ())), preferred_element_type=F32
        )
        return silu_of_half(s * HALF_SCALE), q_rows, k_rows, t, n

    def add(w, q_rows, k_rows):
        acc[q_rows, :] += jnp.dot(w.astype(BF), kv[k_rows, HDIM:], preferred_element_type=F32)

    def full_tiles(i, carry):
        for u in range(4):
            w, q_rows, k_rows, _, _ = scores(full_list[4 * i + u])
            add(w, q_rows, k_rows)
        return carry

    lax.fori_loop(0, full_list[LIST - 1], full_tiles, 0)

    def edge_tiles(i, carry):
        for u in range(2):
            entry = edge_list[2 * i + u]
            w, q_rows, k_rows, t, n = scores(entry)
            first = query_first(info, t)
            col = key_first(info, n) + lax.broadcasted_iota(jnp.int32, (1, KEYS), 1)
            ends = jnp.full((1, KEYS), FAR, jnp.int32)
            for j in range(8):
                e = info[4 + j]
                ends = jnp.minimum(ends, jnp.where(col < e, e, FAR))
            row = lax.broadcasted_iota(jnp.int32, (SUB, KEYS), 0)
            skip = (entry >> 9) * FAR
            allowed = (row >= col + (skip - first)) & (row < ends - first)
            add(jnp.where(allowed, w, 0.0), q_rows, k_rows)
        return carry

    lax.fori_loop(0, edge_list[LIST - 1], edge_tiles, 0)


def early_kernel(info, full_list, edge_list, *refs):
    q_refs, kv_refs = refs[:3], refs[3:9]
    acc, q, kv = refs[9:]
    for e, ref in zip((0, 1, 3), q_refs):
        place_queries(info, e, ref, q)
    for i, ref in enumerate(kv_refs):
        place_keys(info, (0, 1, 3)[i >> 1], i & 1, ref, kv)
    acc[...] = jnp.zeros(acc.shape, F32)
    add_tiles(info, full_list, edge_list, q, kv, acc)


HELD = (((TILES * SUB, HDIM), F32), ((TILES * SUB, HDIM), BF), ((TILES * SUB, 2 * HDIM), BF))


def attend_early(info, lists, queries, keyvals):
    return call(early_kernel, (info, *lists), (*queries, *keyvals), HELD, 4)


def late_kernel(info, full_list, edge_list, acc_in, q_in, kv_in, far_q, near, away, out, acc, q, kv):
    place_queries(info, 2, far_q, q)
    place_keys(info, 2, 0, near, kv)
    place_keys(info, 2, 1, away, kv)
    add_tiles(info, full_list, edge_list, q, kv, acc)
    for t in range(TILES):
        out[t] = acc[t * SUB : (t + 1) * SUB, :].astype(BF)


def attend_late(info, lists, held, far_q, near, away):
    outs = (((TILES, SUB, HDIM), BF), *HELD)
    arrays = (*held, far_q, near, away)
    return call(late_kernel, (info, *lists), arrays, outs, 4, aliases={3: 1, 4: 2, 5: 3})[0]


def gate_kernel(info, part_ref, gate_own, gate_other, own_ref, other_ref):
    ones = jnp.ones((8, HDIM), BF)
    add_lanes = lambda v: lax.dot_general(ones, v, (((1,), (1,)), ((), ())), preferred_element_type=F32)
    for gate_ref, out, rel in ((gate_own, own_ref, 0), (gate_other, other_ref, 1)):
        high, low = [], []
        for half in range(2):
            a = ((2 * rel + half) ^ (2 * info[1])) * 4
            total = part_ref[a].astype(F32)
            for b in range(1, 4):
                total = total + part_ref[a + b].astype(F32)
            at = slice(half * SUB, (half + 1) * SUB)
            out[at, :] = (total * gate_ref[at, :].astype(F32)).astype(BF)
            square = total * total
            top = square.astype(BF)
            sums = add_lanes(top) + add_lanes((square - top.astype(F32)).astype(BF))
            for c in range(SUB // HDIM):
                value = sums[0:1, c * HDIM : (c + 1) * HDIM]
                top = value.astype(BF).astype(F32)
                high.append(top)
                low.append(value - top)
        out[ROWS:, :] = jnp.concatenate(high + low + [jnp.zeros((4, HDIM), F32)], axis=0).astype(BF)


def gate_rows(info, parts, gate_own, gate_other):
    outs = [((ROWS + TAIL, HDIM), BF)] * 2
    return call(gate_kernel, (info,), (parts, gate_own, gate_other), outs, 8)


def mix_kernel(info, *refs):
    rows, w_here, w_there = refs[:4], refs[4], refs[5]
    mine_ref, theirs_ref, squares_ref = refs[6:]
    core = info[3] & 1
    for out, c in ((theirs_ref, 1 - core), (mine_ref, core)):
        cols = pl.ds(pl.multiple_of(c * 256, 256), 256)
        acc = None
        for r, w, flip in zip(rows, (w_here, w_here, w_there, w_there), (0, 1, 1, 0)):
            at = pl.ds(pl.multiple_of((info[1] ^ flip) * HDIM, HDIM), HDIM)
            part = jnp.dot(r[0:ROWS, :], w[at, cols], preferred_element_type=F32)
            acc = part if acc is None else acc + part
        out[0:ROWS, :] = acc.astype(out.dtype)
    tail = sum(r[ROWS:, :].astype(F32) for r in rows)
    squares = jnp.concatenate([tail[0:6] + tail[6:12], jnp.zeros((2, HDIM), F32)], axis=0)
    squares_ref[...] = squares
    top = squares.astype(BF)
    theirs_ref[ROWS : ROWS + 8, 0:HDIM] = top
    theirs_ref[ROWS : ROWS + 8, HDIM:] = (squares - top.astype(F32)).astype(BF)
    theirs_ref[ROWS + 8 :, :] = jnp.zeros((8, 256), BF)


def mix(info, gated, w_here, w_there):
    outs = [((ROWS, 256), F32), ((ROWS + TAIL, 256), BF), ((8, HDIM), F32)]
    return call(mix_kernel, (info,), (*gated, w_here, w_there), outs, 12)


def finish_kernel(mine_ref, got_ref, squares_ref, ev_ref, out_ref, rows, sem):
    tail = got_ref[ROWS : ROWS + 8, :].astype(F32)
    inv = lax.rsqrt((squares_ref[...] + tail[:, 0:HDIM] + tail[:, HDIM:]) * (1.0 / D) + EPS)
    eye = lax.broadcasted_iota(jnp.int32, (HDIM, HDIM), 0) == lax.broadcasted_iota(jnp.int32, (HDIM, HDIM), 1)
    copies = []
    for k in range(6):
        column = jnp.sum(jnp.where(eye, inv[k : k + 1, :], 0.0), axis=1, keepdims=True)
        at = slice(k * HDIM, (k + 1) * HDIM)
        total = mine_ref[at, :] + got_ref[at, :].astype(F32)
        rows[at, :] = (ev_ref[at, :].astype(F32) + total * column).astype(BF)
        copies.append(pltpu.make_async_copy(rows.at[at], out_ref.at[at], sem.at[k]))
        copies[-1].start()
    for c in copies:
        c.wait()


def finish(mine, got, squares, events):
    arrays = [pltpu.with_memory_space_constraint(a, pltpu.VMEM) for a in (mine, got, squares, events)]
    return pl.pallas_call(
        finish_kernel,
        in_specs=[VMEM] * 4,
        out_specs=pl.BlockSpec(memory_space=pl.ANY),
        out_shape=jax.ShapeDtypeStruct((ROWS, 256), BF),
        scratch_shapes=[pltpu.VMEM((ROWS, 256), BF), pltpu.SemaphoreType.DMA((6,))],
        compiler_params=pltpu.CompilerParams(vmem_limit_bytes=8 << 20),
        name="finish",
    )(*arrays)


def layer(events, norm_gain, w_uvqk, w_out, lengths):
    z, yl, x = (lax.axis_index(a).astype(jnp.int32) for a in ("z", "yl", "x"))
    yh = lax.axis_index("yh").astype(jnp.int32)
    o = yh * 2 + lax.axis_index("core").astype(jnp.int32)
    info = jnp.concatenate([jnp.stack([z, yl, x, o]), jnp.cumsum(lengths).astype(jnp.int32)])

    p1, p2 = to_p1(events), to_p2(events)
    c0 = flip_core(events)
    w_in = w_uvqk.reshape(D, 4 * 256)
    gain = norm_gain.reshape(4, 256)
    w_here = lax.dynamic_slice_in_dim(w_out, yh * 512, 512, 1)
    w_away = lax.dynamic_slice_in_dim(w_out, (1 - yh) * 512, 512, 1)
    p1, w_in, info, gain, w_here, w_away = lax.optimization_barrier((p1, w_in, info, gain, w_here, w_away))
    far = [to_p2(p1[:SUB]), to_p1(p2[SUB:])]
    c1, c2 = flip_core(p1), flip_core(p2)
    far_core = [flip_core(far[0]), flip_core(far[1])]

    gate_other, q_other, kv_other, w_in = project_other(info, (p1, c1, p2, c2), gain, w_in)
    gate_own, kv_own, *pieces = project_own(info, (events, c0, *far, *far_core), gain, w_in, q_other)

    pieces = [pieces[0]] + [shift_z(pieces[d], d) for d in (1, 2, 3)]
    up_other, down_other = shift_z(kv_other, 1), shift_z(kv_other, -1)
    up_own, down_own = shift_z(kv_own, 1), shift_z(kv_own, -1)

    q_mine = jnp.concatenate(pieces, axis=0)
    queries = [q_mine] + [shift_x(q_mine, e) for e in (1, 3, 2)]
    near, away = shift_z(up_own, 1), shift_z(down_other, -1)

    keyvals = [kv_own, kv_other, up_own, up_other, down_own, down_other]
    lists = plan(info)
    held = attend_early(info, lists[:2], queries[:3], keyvals)
    parts = attend_late(info, lists[2:], held, queries[3], near, away)

    w_there = to_p3(w_away)

    parts = lax.all_to_all(parts, ("z", "x"), 0, 0)
    own, other = gate_rows(info, parts, gate_own, gate_other)
    gated = [own, to_p1(other), to_p2(other), to_p3(own)]
    mine, theirs, squares = mix(info, gated, w_here, w_there)
    return finish(mine, flip_core(theirs), squares, events)


def solution(mesh):
    fine = Mesh(mesh.devices.reshape(SIZES), AXES)
    ctx, head = ("z", "yl", "x"), ("yh", "core")
    in_specs = (P(ctx, head), P(), P(None, None, head), P(head, None), P())
    return jax.shard_map(layer, mesh=fine, in_specs=in_specs, out_specs=P(ctx, head), check_vma=False)
```

```python
import jax
import jax.numpy as jnp
import numpy as np
from jax import lax
from jax.experimental import pallas as pl
from jax.experimental.pallas import tpu as pltpu
from jax.sharding import Mesh
from jax.sharding import PartitionSpec as P


D = 1024
HDIM = 128
ROWS = 768
SUB = 384
TILES = 16
KEYS = 256
KEY_TILES = 24
TAIL = 16
EPS = 1e-05
AXES = ("z", "yl", "x", "yh", "core")
SIZES = (4, 2, 4, 2, 2)
HALF_SCALE = 0.5 * HDIM ** (-0.5)
FAR = 1 << 24
BF = jnp.bfloat16
F32 = jnp.float32


def send(array, target):
    pairs = []
    for source in range(int(np.prod(SIZES))):
        place = np.unravel_index(source, SIZES)
        dest = [int(t) % n for t, n in zip(target(*[int(p) for p in place]), SIZES)]
        pairs.append((source, int(np.ravel_multi_index(dest, SIZES))))
    return lax.ppermute(array, AXES, pairs)


def flip_core(array):
    return send(array, lambda z, yl, x, yh, c: (z, yl, x, yh, 1 - c))


def to_p1(array):
    return send(array, lambda z, yl, x, yh, c: (z, 1 - yl, x, yh, c))


def to_p2(array):
    return send(array, lambda z, yl, x, yh, c: (z, 1 - yl, x, 1 - yh, c))


def to_p3(array):
    return send(array, lambda z, yl, x, yh, c: (z, yl, x, 1 - yh, c))


def shift_z(array, d):
    return send(array, lambda z, yl, x, yh, c: (z + d, yl, x, yh, c))


def shift_x(array, d):
    return send(array, lambda z, yl, x, yh, c: (z, yl, x + d, yh, c))


def silu_of_half(h):
    return h + h * jnp.tanh(h)


SMEM = pl.BlockSpec(memory_space=pltpu.SMEM)
VMEM = pl.BlockSpec(memory_space=pltpu.VMEM)


def call(kernel, scalars, arrays, outs, limit, scratch=(), aliases={}):
    arrays = [pltpu.with_memory_space_constraint(a, pltpu.VMEM) for a in arrays]
    return pl.pallas_call(
        kernel,
        in_specs=[SMEM] * len(scalars) + [VMEM] * len(arrays),
        out_specs=[VMEM] * len(outs),
        out_shape=[pltpu.VMEM(shape, dtype) for shape, dtype in outs],
        scratch_shapes=list(scratch),
        input_output_aliases=aliases,
        compiler_params=pltpu.CompilerParams(vmem_limit_bytes=limit << 20),
    )(*scalars, *arrays)


PIECE = 128
PER = 3


def project_rows(info, blocks, gain_ref, w_ref, put, offset=0, rows=ROWS):
    gains = [gain_ref[pl.ds(info[3] ^ j, 1), :] for j in range(4)]

    def step(i, carry):
        for r in range(PER):
            here = (PER * i + r) * PIECE + offset
            at = pl.ds(pl.multiple_of(here, PIECE), PIECE)
            xs = [p[pl.ds(pl.multiple_of(here - f, PIECE), PIECE), :].astype(F32) for p, f in blocks]
            total = sum(jnp.sum(v, axis=1, keepdims=True) for v in xs)
            mean = total * (1.0 / D)
            xs = [v - mean for v in xs]
            var = sum(jnp.sum(v * v, axis=1, keepdims=True) for v in xs) * (1.0 / D)
            inv = lax.rsqrt(var + EPS)
            acc = None
            for j, v in enumerate(xs):
                n = (v * inv * gains[j]).astype(BF)
                part = jnp.dot(n, w_ref[j * 256 : (j + 1) * 256, :], preferred_element_type=F32)
                acc = part if acc is None else acc + part
            put(at, silu_of_half(acc * 0.5).astype(BF))
        return carry

    lax.fori_loop(0, rows // PIECE // PER, step, 0)


def put_into(gate_ref, q_ref, kv_ref):
    def put(at, y):
        gate_ref[at, :] = y[:, :128]
        q_ref[at, :] = y[:, 256:384]
        kv_ref[at, :128] = y[:, 384:]
        kv_ref[at, 128:] = y[:, 128:256]

    return put


def other_kernel(info, *refs):
    blocks, gain_ref, w_ref = refs[:4], refs[4], refs[5]
    gate_ref, q_ref, kv_ref, w_out = refs[6:]
    for j in range(4):
        rows = pl.ds(pl.multiple_of((info[3] ^ j) * 256, 256), 256)
        for g in range(4):
            cols = pl.ds(pl.multiple_of(g * 256 + info[1] * HDIM, HDIM), HDIM)
            w_out[j * 256 : (j + 1) * 256, g * HDIM : (g + 1) * HDIM] = w_ref[rows, cols]
    project_rows(info, [(b, 0) for b in blocks], gain_ref, w_out, put_into(gate_ref, q_ref, kv_ref))


def own_kernel(info, *refs):
    here, core, far, far_core = refs[0], refs[1], refs[2:4], refs[4:6]
    gain_ref, w_ref, q_other = refs[6:9]
    gate_ref, kv_ref, q_refs, q_own = refs[9], refs[10], refs[11:15], refs[15]
    put = put_into(gate_ref, q_own, kv_ref)
    for half in range(2):
        at = half * SUB
        blocks = [(here, 0), (core, 0), (far[half], at), (far_core[half], at)]
        project_rows(info, blocks, gain_ref, w_ref, put, at, SUB)
    for i in range(4):
        source = (q_own, q_other)[i >> 1]
        shift = lax.rem((i ^ (2 * info[1])) - info[0] + 4, 4)
        for d in range(4):

            @pl.when(shift == d)
            def _():
                q_refs[d][...] = source[(i & 1) * SUB : ((i & 1) + 1) * SUB, :]


def project_other(info, blocks, gain, w):
    outs = [((ROWS, HDIM), BF), ((ROWS, HDIM), BF), ((ROWS, 2 * HDIM), BF), ((D, 4 * HDIM), BF)]
    return call(other_kernel, (info,), (*blocks, gain, w), outs, 8)


def project_own(info, blocks, gain, w, q_other):
    outs = [((ROWS, HDIM), BF), ((ROWS, 2 * HDIM), BF)] + [((SUB, HDIM), BF)] * 4
    scratch = [pltpu.VMEM((ROWS, HDIM), BF)]
    return call(own_kernel, (info,), (*blocks, gain, w, q_other), outs, 8, scratch)


LIST = 416


def plan_kernel(info, full_early, edge_early, full_late, edge_late):
    z, yl, x = info[0], info[1], info[2]
    far_z, far_x = lax.rem(z + 2, 4), lax.rem(x + 2, 4)

    def start_of(position):
        s = jnp.int32(0)
        for i in range(8):
            e = info[4 + i]
            s = jnp.maximum(s, jnp.where(e <= position, e, 0))
        return s

    def tiles_upto(position):
        t = position - x * ROWS
        m = lax.div(t, 4 * ROWS)
        r = lax.div(t - m * (4 * ROWS), KEYS)
        count = 3 * m + 1 + jnp.minimum(r, 2)
        return jnp.minimum(jnp.where(t < 0, 0, count), KEY_TILES)

    def list_queries(t, counts):
        first = query_first(info, t)
        begin_last = start_of(first + SUB - 1)
        low = tiles_upto(start_of(first) - KEYS)
        high = tiles_upto(first + SUB - 1)
        near = (t & 3) != far_x

        def list_keys(n, counts):
            fe, ee, fl, el = counts
            k = key_first(info, n)
            early = near & (lax.div(n, 6) != far_z)
            full = (k + KEYS - 1 <= first) & (k >= begin_last)
            entry = t * 32 + n
            full_early[fe] = entry
            edge_early[ee] = entry
            full_late[fl] = entry
            edge_late[el] = entry
            early, full = early.astype(jnp.int32), full.astype(jnp.int32)
            return (
                fe + early * full,
                ee + early * (1 - full),
                fl + (1 - early) * full,
                el + (1 - early) * (1 - full),
            )

        return lax.fori_loop(low, high, list_keys, counts)

    zero = jnp.int32(0)
    fe, ee, fl, el = lax.fori_loop(0, TILES, list_queries, (zero, zero, zero, zero))
    for fulls, nf, edges, ne in ((full_early, fe, edge_early, ee), (full_late, fl, edge_late, el)):
        groups = nf >> 3

        def move(i, ne):
            edges[ne] = fulls[i]
            return ne + 1

        ne = lax.fori_loop(groups * 8, nf, move, ne)
        for pad in range(2):
            edges[ne + pad] = 512 + (z * 4 + x) * 32 + z * 6 + 3 * yl
        fulls[LIST - 1] = groups
        edges[LIST - 1] = lax.div(ne + 2, 3)


def query_first(info, t):
    return ((t >> 2) * 8 + (info[0] >> 1) * 4 + (t & 3)) * ROWS + (info[0] & 1) * SUB


def key_first(info, n):
    m = lax.div(n, 3)
    return (m * 4 + info[2]) * ROWS + (n - 3 * m) * KEYS


def plan(info):
    return pl.pallas_call(
        plan_kernel,
        in_specs=[SMEM],
        out_specs=[SMEM] * 4,
        out_shape=[jax.ShapeDtypeStruct((LIST,), jnp.int32)] * 4,
        compiler_params=pltpu.CompilerParams(vmem_limit_bytes=1 << 20),
        name="plan",
    )(info)


def place_queries(info, e, ref, q):
    for k in range(4):
        tile = lax.rem(info[0] - k + 4, 4) * 4 + lax.rem(info[2] - e + 4, 4)
        q[pl.ds(pl.multiple_of(tile * SUB, SUB), SUB), :] = ref[k * SUB : (k + 1) * SUB, :]


def place_keys(info, d, rel, ref, kv):
    block = lax.rem(info[0] - d + 4, 4) * 2 + (info[1] ^ rel)
    kv[pl.ds(pl.multiple_of(block * ROWS, ROWS), ROWS), :] = ref[...]


def add_tiles(info, full_list, edge_list, q, kv, acc):
    def scores(entry):
        t, n = (entry >> 5) & 15, entry & 31
        q_rows = pl.ds(pl.multiple_of(t * SUB, SUB), SUB)
        k_rows = pl.ds(pl.multiple_of(n * KEYS, KEYS), KEYS)
        s = lax.dot_general(
            q[q_rows, :], kv[k_rows, 0:HDIM], (((1,), (1,)), ((), ())), preferred_element_type=F32
        )
        return silu_of_half(s * HALF_SCALE), q_rows, k_rows, t, n

    def add(w, q_rows, k_rows):
        acc[q_rows, :] += jnp.dot(w.astype(BF), kv[k_rows, HDIM:], preferred_element_type=F32)

    def full_tiles(i, carry):
        for u in range(8):
            w, q_rows, k_rows, _, _ = scores(full_list[8 * i + u])
            add(w, q_rows, k_rows)
        return carry

    lax.fori_loop(0, full_list[LIST - 1], full_tiles, 0)

    def edge_tiles(i, carry):
        for u in range(3):
            entry = edge_list[3 * i + u]
            w, q_rows, k_rows, t, n = scores(entry)
            first = query_first(info, t)
            col = key_first(info, n) + lax.broadcasted_iota(jnp.int32, (1, KEYS), 1)
            ends = jnp.full((1, KEYS), FAR, jnp.int32)
            for j in range(8):
                e = info[4 + j]
                ends = jnp.minimum(ends, jnp.where(col < e, e, FAR))
            row = lax.broadcasted_iota(jnp.int32, (SUB, KEYS), 0)
            skip = (entry >> 9) * FAR
            allowed = (row >= col + (skip - first)) & (row < ends - first)
            add(jnp.where(allowed, w, 0.0), q_rows, k_rows)
        return carry

    lax.fori_loop(0, edge_list[LIST - 1], edge_tiles, 0)


def early_kernel(info, full_list, edge_list, *refs):
    q_refs, kv_refs = refs[:3], refs[3:9]
    acc, q, kv = refs[9:]
    for e, ref in zip((0, 1, 3), q_refs):
        place_queries(info, e, ref, q)
    for i, ref in enumerate(kv_refs):
        place_keys(info, (0, 1, 3)[i >> 1], i & 1, ref, kv)
    acc[...] = jnp.zeros(acc.shape, F32)
    add_tiles(info, full_list, edge_list, q, kv, acc)


HELD = (((TILES * SUB, HDIM), F32), ((TILES * SUB, HDIM), BF), ((TILES * SUB, 2 * HDIM), BF))


def attend_early(info, lists, queries, keyvals):
    return call(early_kernel, (info, *lists), (*queries, *keyvals), HELD, 4)


def late_kernel(info, full_list, edge_list, acc_in, q_in, kv_in, far_q, near, away, out, acc, q, kv):
    place_queries(info, 2, far_q, q)
    place_keys(info, 2, 0, near, kv)
    place_keys(info, 2, 1, away, kv)
    add_tiles(info, full_list, edge_list, q, kv, acc)
    for t in range(TILES):
        out[t] = acc[t * SUB : (t + 1) * SUB, :].astype(BF)


def attend_late(info, lists, held, far_q, near, away):
    outs = (((TILES, SUB, HDIM), BF), *HELD)
    arrays = (*held, far_q, near, away)
    return call(late_kernel, (info, *lists), arrays, outs, 4, aliases={3: 1, 4: 2, 5: 3})[0]


def gate_kernel(info, part_ref, gate_own, gate_other, own_ref, other_ref):
    ones = jnp.ones((8, HDIM), BF)
    add_lanes = lambda v: lax.dot_general(ones, v, (((1,), (1,)), ((), ())), preferred_element_type=F32)
    for gate_ref, out, rel in ((gate_own, own_ref, 0), (gate_other, other_ref, 1)):
        high, low = [], []
        for half in range(2):
            a = ((2 * rel + half) ^ (2 * info[1])) * 4
            total = part_ref[a].astype(F32)
            for b in range(1, 4):
                total = total + part_ref[a + b].astype(F32)
            at = slice(half * SUB, (half + 1) * SUB)
            out[at, :] = (total * gate_ref[at, :].astype(F32)).astype(BF)
            square = total * total
            top = square.astype(BF)
            sums = add_lanes(top) + add_lanes((square - top.astype(F32)).astype(BF))
            for c in range(SUB // HDIM):
                value = sums[0:1, c * HDIM : (c + 1) * HDIM]
                top = value.astype(BF).astype(F32)
                high.append(top)
                low.append(value - top)
        out[ROWS:, :] = jnp.concatenate(high + low + [jnp.zeros((4, HDIM), F32)], axis=0).astype(BF)


def gate_rows(info, parts, gate_own, gate_other):
    outs = [((ROWS + TAIL, HDIM), BF)] * 2
    return call(gate_kernel, (info,), (parts, gate_own, gate_other), outs, 8)


def mix_kernel(info, *refs):
    rows, w_here, w_there = refs[:4], refs[4], refs[5]
    mine_ref, theirs_ref, squares_ref = refs[6:]
    core = info[3] & 1
    for out, c in ((theirs_ref, 1 - core), (mine_ref, core)):
        cols = pl.ds(pl.multiple_of(c * 256, 256), 256)
        acc = None
        for r, w, flip in zip(rows, (w_here, w_here, w_there, w_there), (0, 1, 1, 0)):
            at = pl.ds(pl.multiple_of((info[1] ^ flip) * HDIM, HDIM), HDIM)
            part = jnp.dot(r[0:ROWS, :], w[at, cols], preferred_element_type=F32)
            acc = part if acc is None else acc + part
        out[0:ROWS, :] = acc.astype(out.dtype)
    tail = sum(r[ROWS:, :].astype(F32) for r in rows)
    squares = jnp.concatenate([tail[0:6] + tail[6:12], jnp.zeros((2, HDIM), F32)], axis=0)
    squares_ref[...] = squares
    top = squares.astype(BF)
    theirs_ref[ROWS : ROWS + 8, 0:HDIM] = top
    theirs_ref[ROWS : ROWS + 8, HDIM:] = (squares - top.astype(F32)).astype(BF)
    theirs_ref[ROWS + 8 :, :] = jnp.zeros((8, 256), BF)


def mix(info, gated, w_here, w_there):
    outs = [((ROWS, 256), F32), ((ROWS + TAIL, 256), BF), ((8, HDIM), F32)]
    return call(mix_kernel, (info,), (*gated, w_here, w_there), outs, 12)


def finish_kernel(mine_ref, got_ref, squares_ref, ev_ref, out_ref, rows, sem):
    tail = got_ref[ROWS : ROWS + 8, :].astype(F32)
    inv = lax.rsqrt((squares_ref[...] + tail[:, 0:HDIM] + tail[:, HDIM:]) * (1.0 / D) + EPS)
    eye = lax.broadcasted_iota(jnp.int32, (HDIM, HDIM), 0) == lax.broadcasted_iota(jnp.int32, (HDIM, HDIM), 1)
    copies = []
    for k in range(6):
        column = jnp.sum(jnp.where(eye, inv[k : k + 1, :], 0.0), axis=1, keepdims=True)
        at = slice(k * HDIM, (k + 1) * HDIM)
        total = mine_ref[at, :] + got_ref[at, :].astype(F32)
        rows[at, :] = (ev_ref[at, :].astype(F32) + total * column).astype(BF)
        copies.append(pltpu.make_async_copy(rows.at[at], out_ref.at[at], sem.at[k]))
        copies[-1].start()
    for c in copies:
        c.wait()


def finish(mine, got, squares, events):
    arrays = [pltpu.with_memory_space_constraint(a, pltpu.VMEM) for a in (mine, got, squares, events)]
    return pl.pallas_call(
        finish_kernel,
        in_specs=[VMEM] * 4,
        out_specs=pl.BlockSpec(memory_space=pl.ANY),
        out_shape=jax.ShapeDtypeStruct((ROWS, 256), BF),
        scratch_shapes=[pltpu.VMEM((ROWS, 256), BF), pltpu.SemaphoreType.DMA((6,))],
        compiler_params=pltpu.CompilerParams(vmem_limit_bytes=8 << 20),
        name="finish",
    )(*arrays)


def layer(events, norm_gain, w_uvqk, w_out, lengths):
    z, yl, x = (lax.axis_index(a).astype(jnp.int32) for a in ("z", "yl", "x"))
    yh = lax.axis_index("yh").astype(jnp.int32)
    o = yh * 2 + lax.axis_index("core").astype(jnp.int32)
    info = jnp.concatenate([jnp.stack([z, yl, x, o]), jnp.cumsum(lengths).astype(jnp.int32)])

    p1, p2 = to_p1(events), to_p2(events)
    c0 = flip_core(events)
    w_in = w_uvqk.reshape(D, 4 * 256)
    gain = norm_gain.reshape(4, 256)
    w_here = lax.dynamic_slice_in_dim(w_out, yh * 512, 512, 1)
    w_away = lax.dynamic_slice_in_dim(w_out, (1 - yh) * 512, 512, 1)
    p1, w_in, info, gain, w_here, w_away = lax.optimization_barrier((p1, w_in, info, gain, w_here, w_away))
    far = [to_p2(p1[:SUB]), to_p1(p2[SUB:])]
    c1, c2 = flip_core(p1), flip_core(p2)
    far_core = [flip_core(far[0]), flip_core(far[1])]

    gate_other, q_other, kv_other, w_in = project_other(info, (p1, c1, p2, c2), gain, w_in)
    gate_own, kv_own, *pieces = project_own(info, (events, c0, *far, *far_core), gain, w_in, q_other)

    pieces = [pieces[0]] + [shift_z(pieces[d], d) for d in (1, 2, 3)]
    up_other, down_other = shift_z(kv_other, 1), shift_z(kv_other, -1)
    up_own, down_own = shift_z(kv_own, 1), shift_z(kv_own, -1)

    q_mine = jnp.concatenate(pieces, axis=0)
    queries = [q_mine] + [shift_x(q_mine, e) for e in (1, 3, 2)]
    near, away = shift_z(up_own, 1), shift_z(down_other, -1)

    keyvals = [kv_own, kv_other, up_own, up_other, down_own, down_other]
    lists = plan(info)
    held = attend_early(info, lists[:2], queries[:3], keyvals)
    parts = attend_late(info, lists[2:], held, queries[3], near, away)

    w_there = to_p3(w_away)

    parts = lax.all_to_all(parts, ("z", "x"), 0, 0)
    own, other = gate_rows(info, parts, gate_own, gate_other)
    gated = [own, to_p1(other), to_p2(other), to_p3(own)]
    mine, theirs, squares = mix(info, gated, w_here, w_there)
    return finish(mine, flip_core(theirs), squares, events)


def solution(mesh):
    fine = Mesh(mesh.devices.reshape(SIZES), AXES)
    ctx, head = ("z", "yl", "x"), ("yh", "core")
    in_specs = (P(ctx, head), P(), P(None, None, head), P(head, None), P())
    return jax.shard_map(layer, mesh=fine, in_specs=in_specs, out_specs=P(ctx, head), check_vma=False)
```
